128 devices in a mesh: dp: 4 (over z_lo, core), tensor: 32 (over x, z_hi, y).
Axes of the slice: x: 4, y: 4, z: 4 (z_hi: 2, z_lo: 2; z = z_hi * 2 + z_lo), core: 2. Of those that a mesh axis runs over, the one named last changes fastest.
Arguments:
- hidden: bfloat16 [2048, 4096], P('dp'), may hold values from -6 to 6
- segment_ids: int32 [2048], P('dp'), may hold values from 0 to 31, as said below
- first_gain: float32 [4096], replicated, may hold values from 0.1 to 1.9
- second_gain: float32 [4096], replicated, may hold values from 0.1 to 1.9
- qkv_master: float32 [4096, 3, 4096], P(('dp', 'tensor'))
- out_master: float32 [4096, 4096], P(None, ('dp', 'tensor')), may hold values from -0.09375 to 0.09375
- up_master: float32 [4096, 16384], P(('dp', 'tensor')), may hold values from -0.09375 to 0.09375
- down_master: float32 [16384, 4096], P(None, ('dp', 'tensor')), may hold values from -0.046875 to 0.046875
Outputs:
- new_hidden: bfloat16 [2048, 4096], P(('dp', 'tensor'))
- key_cache: bfloat16 [2048, 4096], P('dp', 'tensor')
- value_cache: bfloat16 [2048, 4096], P('dp', 'tensor')
- qkv_block: bfloat16 [4096, 3, 4096], P(None, None, 'tensor')
- out_block: bfloat16 [4096, 4096], P('tensor')
- up_block: bfloat16 [4096, 16384], P(None, 'tensor')
- down_block: bfloat16 [16384, 4096], P('tensor')
The draws below stay inside these ranges and needn't reach their ends.
Inputs may be any that keep to these rules, and one draw needn't show every extreme that they name: `segment_ids`: never falls along the tokens; group g holds exactly the 8 prompts 8 g to 8 g + 7, each of 1 to 505 tokens, and in some group one prompt has exactly 505 tokens.
All inputs are finite; a program needn't handle non-finite values.
Results may differ from the reference program's by a relative error of at most 0.029.
Values may be sent and summed in bfloat16 or wider, within the bound.
A program may use at most 128 MiB of HBM per device.

```python
import math
import jax
import jax.numpy as jnp
from jax import lax

D = 4096
FF = 16384
HD = 128
TOK_GRP = 512
TOKENS = 2048
N_DP = 4
N_TENSOR = 32


def draw_qkv_master(key, part):
    first_key = jax.random.fold_in(jax.random.fold_in(key, 17), 0)
    base = jax.random.normal(first_key, (D, 3, D), jnp.float32) / math.sqrt(D)
    return base


def draw_segment_ids(key, part):
    group_count = TOKENS // TOK_GRP
    pick_key, long_key, cut_key = jax.random.split(jax.random.fold_in(key, 29), 3)
    chosen = jax.random.randint(pick_key, (), 0, group_count)
    long_at = jax.random.randint(long_key, (), 0, 8)

    def cuts_of(index):
        shuffled = jax.random.permutation(jax.random.fold_in(cut_key, index), TOK_GRP - 1) + 1
        return jnp.sort(shuffled[:7]).astype(jnp.int32)
    random_cuts = jax.vmap(cuts_of)(jnp.arange(group_count))
    order = jnp.arange(1, 8).astype(jnp.int32)
    forced = jnp.where(order <= long_at, order, order + TOK_GRP - 8).astype(jnp.int32)
    is_chosen = (jnp.arange(group_count) == chosen)[:, None]
    cuts = jnp.where(is_chosen, forced[None, :], random_cuts)
    place = jnp.arange(TOK_GRP).astype(jnp.int32)
    inner = jnp.sum((cuts[:, None, :] <= place[None, :, None]).astype(jnp.int32), axis=-1)
    labels = inner + 8 * jnp.arange(group_count).astype(jnp.int32)[:, None]
    return labels.reshape(TOKENS).astype(jnp.int32)


def level_of(stream_key, shape, shards, low, largest):
    def one(dim, parts):
        steps = jax.random.uniform(jax.random.fold_in(jax.random.fold_in(stream_key, 6), dim), (parts,), jnp.float32, low / len(shards), largest / len(shards))
        return jnp.repeat(jnp.exp(steps), shape[dim] // parts).reshape((-1,) + (1,) * (len(shape) - dim - 1))

    level = one(*shards[0])
    for cut in shards[1:]:
        level = level * one(*cut)
    return level


def normal_values(stream_key, shape, scale, reach, cuts=(), kind=jnp.bfloat16):
    entries = jax.random.normal(stream_key, shape, jnp.float32) * scale
    if len(cuts) > 0:
        entries = level_of(stream_key, shape, cuts, -0.22, 0.18) * entries
    return jnp.clip(entries, min=-reach, max=reach).astype(kind)


def setup_inputs(seed: int = 0) -> dict:
    streams_of = jax.random.split(jax.random.key(seed), 9)
    return {
        "hidden": normal_values(streams_of[0], (TOKENS, D), 1.0, 6.0, ((0, 4),)),
        "segment_ids": draw_segment_ids(jax.random.fold_in(streams_of[8], 71), 0),
        "first_gain": jnp.clip(1.0 + 0.18 * jax.random.normal(streams_of[2], (D,), jnp.float32), 0.1, 1.9),
        "second_gain": jnp.clip(1.0 + 0.18 * jax.random.normal(streams_of[3], (D,), jnp.float32), 0.1, 1.9),
        "qkv_master": draw_qkv_master(jax.random.fold_in(streams_of[8], 71), 0),
        "out_master": normal_values(streams_of[5], (D, D), D ** -0.5, 0.09375, ((1, 128),), jnp.float32),
        "up_master": normal_values(streams_of[6], (D, FF), D ** -0.5, 0.09375, ((0, 128),), jnp.float32),
        "down_master": normal_values(streams_of[7], (FF, D), FF ** -0.5, 0.046875, ((1, 128),), jnp.float32),
    }


EPSILON = 1e-05

def layer_norm(values, gain):
    values = values.astype(jnp.float32)
    center = values - lax.optimization_barrier(jnp.mean(values, axis=-1, keepdims=True))
    spread = lax.optimization_barrier(jnp.mean(center * center, axis=-1, keepdims=True))
    return center * lax.rsqrt(spread + EPSILON) * gain

def block_sum(left, right, blocks):
    length = left.shape[0]
    width = left.shape[1] // blocks
    parted = jnp.einsum('gtc,tcd->tgd', left.reshape(length, blocks, width).astype(jnp.float32), right.reshape(blocks, width, right.shape[1]).astype(jnp.float32))
    parted = lax.optimization_barrier(parted.astype(jnp.bfloat16))
    return lax.optimization_barrier(jnp.sum(parted.astype(jnp.float32), axis=0))

def reference(hidden, segment_ids, first_gain, second_gain, qkv_master, out_master, up_master, down_master):
    qkv_block = qkv_master.astype(jnp.bfloat16)
    out_block = out_master.astype(jnp.bfloat16)
    up_block = up_master.astype(jnp.bfloat16)
    down_block = down_master.astype(jnp.bfloat16)
    all_heads = D // HD
    slopes = jnp.exp2(-8.0 * (jnp.arange(all_heads).astype(jnp.float32) + 1.0) / all_heads)
    position = jnp.arange(TOK_GRP)
    distance = (position[:, None] - position[None, :]).astype(jnp.float32)
    outputs, key_list, value_list = ([], [], [])
    for group in range(N_DP):
        tok_rows = hidden[group * TOK_GRP:(group + 1) * TOK_GRP]
        group_ids = segment_ids[group * TOK_GRP:(group + 1) * TOK_GRP]
        normed = layer_norm(tok_rows, first_gain).astype(jnp.bfloat16)
        projected = jnp.einsum('nd,dkc->nkc', normed.astype(jnp.float32), qkv_block.astype(jnp.float32)).astype(jnp.bfloat16)
        queries = projected[:, 0].reshape(TOK_GRP, all_heads, HD).astype(jnp.float32)
        key_rows = projected[:, 1]
        value_rows = projected[:, 2]
        scores = jnp.einsum('qhe,khe->hqk', queries, key_rows.reshape(TOK_GRP, all_heads, HD).astype(jnp.float32)) / math.sqrt(HD)
        scores = scores - slopes[:, None, None] * distance
        allowed = (group_ids[:, None] == group_ids[None, :]) & (distance >= 0)
        scores = jnp.where(allowed, scores, -jnp.inf)
        highest = lax.optimization_barrier(jnp.max(scores, axis=-1, keepdims=True))
        raised = jnp.exp(scores - highest)
        weights = (raised / lax.optimization_barrier(jnp.sum(raised, axis=-1, keepdims=True))).astype(jnp.bfloat16)
        context = jnp.einsum('hqk,khe->qhe', weights.astype(jnp.float32), value_rows.reshape(TOK_GRP, all_heads, HD).astype(jnp.float32)).astype(jnp.bfloat16).reshape(TOK_GRP, D)
        attended = block_sum(context, out_block, N_TENSOR)
        middle = (tok_rows.astype(jnp.float32) + attended).astype(jnp.bfloat16)
        normed_two = layer_norm(middle, second_gain).astype(jnp.bfloat16)
        activated = jax.nn.gelu(jnp.dot(normed_two, up_block, preferred_element_type=jnp.float32), approximate=False).astype(jnp.bfloat16)
        lowered = block_sum(activated, down_block, N_TENSOR)
        outputs.append((middle.astype(jnp.float32) + lowered).astype(jnp.bfloat16))
        key_list.append(key_rows)
        value_list.append(value_rows)
    new_hidden = jnp.concatenate(outputs, axis=0)
    key_cache = jnp.concatenate(key_list, axis=0)
    value_cache = jnp.concatenate(value_list, axis=0)
    return (new_hidden, key_cache, value_cache, qkv_block, out_block, up_block, down_block)
```

```python
import functools
import math

import jax
import jax.numpy as jnp
from jax import lax
from jax.experimental import pallas as pl
from jax.experimental.pallas import tpu as pltpu
from jax.sharding import PartitionSpec as P

D = 4096
HD = 128
EPSILON = 1e-05
MESH = pl.DeviceIdType.MESH
BF16 = jnp.bfloat16
F32 = jnp.float32


def layer_norm(values, gain):
    values = values.astype(F32)
    center = values - jnp.mean(values, axis=-1, keepdims=True)
    spread = jnp.mean(center * center, axis=-1, keepdims=True)
    return center * lax.rsqrt(spread + EPSILON) * gain


class Place:
    def __init__(self):
        self.dp = lax.axis_index("dp")
        self.t = lax.axis_index("tensor")
        self.zl = self.dp // 2
        self.core = self.dp % 2
        self.x = self.t // 8
        self.zh = (self.t // 4) % 2
        self.y = self.t % 4
        self.z_pair = (1 - self.zl) * 2 + self.core
        self.core_pair = self.zl * 2 + (1 - self.core)

    def near(self, axis, delta):
        if axis == "x":
            return (self.dp, ((self.x + delta) % 4) * 8 + self.zh * 4 + self.y)
        return (self.dp, self.x * 8 + self.zh * 4 + (self.y + delta) % 4)

    def across(self):
        return (self.dp, self.x * 8 + (1 - self.zh) * 4 + self.y)


def remote(src, dst, send_sem, recv_sem, device):
    return pltpu.make_async_remote_copy(
        src_ref=src,
        dst_ref=dst,
        send_sem=send_sem,
        recv_sem=recv_sem,
        device_id=device,
        device_id_type=MESH,
    )


def greet(barrier, device):
    pl.semaphore_signal(barrier, inc=1, device_id=device, device_id_type=MESH)


def relay_kernel(
    q_in, o_in, u_in, w_in, qo, upq, dnq, sq, su, sw, local, s_sem, r_sem, fz_s, fz_r, fc_s, fc_r, f3_s, f3_r
):
    me = Place()

    def holder(step):
        other = (me.t + step) % 32
        apart = (me.zh + (other // 4) % 2) % 2
        return other, apart, ((me.zl + apart) % 2) * 2 + me.core

    barrier = pltpu.get_barrier_semaphore()

    def hello(step, carry):
        other, _, group = holder(step)
        greet(barrier, (group, other))
        return carry

    lax.fori_loop(1, 32, hello, 0)
    greet(barrier, (me.z_pair, me.t))
    greet(barrier, (me.core_pair, me.t))

    sq[0:3] = q_in[...].astype(BF16)
    sq[3] = o_in[...].astype(BF16)
    pl.semaphore_wait(barrier, 33)

    mine = me.dp * 8 + me.x * 2 + me.zh
    rows = pl.ds(pl.multiple_of(me.y * 32, 32), 32)

    def send(source, place, index):
        def body(step, carry):
            other, apart, group = holder(step)
            slot = apart * 4 + me.x
            remote(
                source(other), place(slot), s_sem.at[index], r_sem.at[index * 8 + slot], (group, other)
            ).start()
            return carry

        lax.fori_loop(1, 32, body, 0)
        own = pltpu.make_async_copy(source(me.t), place(me.x), local.at[index])
        own.start()
        return own

    def cut(ref, wide):
        return lambda other: ref.at[..., pl.ds(pl.multiple_of(other * wide, wide), wide)]

    own_q = send(cut(sq, 128), lambda slot: qo.at[:, mine, rows, :], 0)

    @pl.loop(0, 4)
    def _(part):
        cols = pl.ds(pl.multiple_of(part * 4096, 4096), 4096)
        su[:, cols] = u_in[:, cols].astype(BF16)

    own_u = send(cut(su, 512), lambda slot: upq.at[slot, rows, :], 1)

    @pl.loop(0, 4)
    def _(part):
        cols = pl.ds(pl.multiple_of(part * 4096, 4096), 4096)
        sw[:, cols] = w_in[:, cols].astype(BF16)

    own_w = send(cut(sw, 512), lambda slot: dnq.at[slot, rows, :], 2)
    own_q.wait()
    own_u.wait()
    own_w.wait()

    def batch(slot, flip_z, flip_c):
        apart = slot // 4
        zl = (me.zl + apart + flip_z) % 2
        core = (me.core + flip_c) % 2
        return (zl * 2 + core) * 8 + (slot % 4) * 2 + (me.zh + apart) % 2

    def wait_pieces(base, row_ref, slot):
        full = row_ref(slot)

        @pl.when(slot != me.x)
        def _():
            remote(full(128), full(128), s_sem.at[0], r_sem.at[base + slot], (me.core_pair, me.t)).wait_recv()

        @pl.when(slot == me.x)
        def _():
            remote(full(96), full(96), s_sem.at[0], r_sem.at[base + slot], (me.core_pair, me.t)).wait_recv()

    def q_rows(slot):
        return lambda count: qo.at[:, batch(slot, 0, 0), pl.ds(0, count), :]

    def to_z(slot):
        ref = qo.at[:, batch(slot, 0, 0)]
        return remote(ref, ref, fz_s.at[slot], fz_r.at[slot], (me.z_pair, me.t))

    def to_core(slot):
        ref = qo.at[:, batch(slot, 0, 0)]
        return remote(ref, ref, fc_s.at[slot], fc_r.at[slot], (me.core_pair, me.t))

    def pass_on(slot):
        ref = qo.at[:, batch(slot, 1, 0)]
        return remote(ref, ref, f3_s.at[slot], f3_r.at[slot], (me.core_pair, me.t))

    def got(slot, flip_z, flip_c, sem):
        ref = qo.at[:, batch(slot, flip_z, flip_c)]
        remote(ref, ref, s_sem.at[0], sem, (me.core_pair, me.t)).wait_recv()

    lag = 2

    def forward(step, carry):
        @pl.when(step < 8)
        def _():
            wait_pieces(0, q_rows, step)
            to_z(step).start()
            to_core(step).start()

        @pl.when(step >= lag)
        def _():
            got(step - lag, 1, 0, fz_r.at[step - lag])
            pass_on(step - lag).start()

        return carry

    lax.fori_loop(0, 8 + lag, forward, 0)

    def finish(slot, carry):
        wait_pieces(8, lambda s: lambda count: upq.at[s, pl.ds(0, count), :], slot)
        wait_pieces(16, lambda s: lambda count: dnq.at[s, pl.ds(0, count), :], slot)
        got(slot, 0, 1, fc_r.at[slot])
        got(slot, 1, 1, f3_r.at[slot])
        to_z(slot).wait_send()
        to_core(slot).wait_send()
        pass_on(slot).wait_send()
        return carry

    lax.fori_loop(0, 8, finish, 0)
    for index, ref, wide in ((0, sq, 128), (1, su, 512), (2, sw, 512)):
        sent = ref.at[..., pl.ds(0, 31 * wide)]
        remote(sent, sent, s_sem.at[index], r_sem.at[0], (me.core_pair, me.t)).wait_send()


def relay(qkv, out, up, down):
    any_spec = pl.BlockSpec(memory_space=pl.ANY)
    dma = pltpu.SemaphoreType.DMA
    return pl.pallas_call(
        relay_kernel,
        out_shape=(
            jax.ShapeDtypeStruct((4, 32, 128, 128), BF16),
            jax.ShapeDtypeStruct((8, 128, 512), BF16),
            jax.ShapeDtypeStruct((8, 128, 512), BF16),
        ),
        in_specs=[pl.BlockSpec(memory_space=pltpu.VMEM)] * 4,
        out_specs=[any_spec] * 3,
        scratch_shapes=[
            pltpu.VMEM((4, 32, 4096), BF16),
            pltpu.VMEM((32, 16384), BF16),
            pltpu.VMEM((32, 16384), BF16),
            dma((3,)),
            dma((3,)),
            dma((24,)),
        ]
        + [dma((8,))] * 6,
        compiler_params=pltpu.CompilerParams(
            collective_id=0, has_side_effects=True, vmem_limit_bytes=48 << 20
        ),
        name="relay",
    )(qkv, out, up, down)


HALF = 2048


def reduce_rows(me, share, bufs, sems):
    ra, acc_a, rb, acc_b, kept, last, last_half, rc = bufs
    sa, qa, sb, qb, sc, qc = sems
    axes = (("x", "y"), ("y", "x"))

    def chunk_a(f, q, h):
        if f == 0:
            return share.at[q, h, :, :, pl.ds(0, HALF)]
        return share.at[:, h, q, :, pl.ds(HALF, HALF)]

    def chunk_b(f, q, h):
        return kept.at[f, q, h]

    def position(axis):
        return me.x if axis == "x" else me.y

    def stage(level, chunk, recv, acc, s_sem, r_sem, store):
        started = []
        plan = []
        for f in range(2):
            axis = axes[f][level]
            p = position(axis)
            far = (p + 2) % 4
            for way in range(2):
                delta = 1 - 2 * way
                near = (p + delta) % 4
                device = me.near(axis, delta)
                first = remote(
                    chunk(f, far, way), recv.at[f, way, 0], s_sem.at[f, way, 0], r_sem.at[f, way, 0], device
                )
                plain = remote(
                    chunk(f, near, 1 - way), recv.at[f, way, 1], s_sem.at[f, way, 1], r_sem.at[f, way, 1], device
                )
                summed = remote(
                    acc.at[f, way], recv.at[f, way, 2], s_sem.at[f, way, 2], r_sem.at[f, way, 2], device
                )
                plan.append((f, way, near, first, plain, summed))
        for f, way, near, first, plain, summed in plan:
            first.start()
        for f, way, near, first, plain, summed in plan:
            plain.start()
        for f, way, near, first, plain, summed in plan:
            first.wait_recv()
            acc[f, way] = (chunk(f, near, way)[...].astype(F32) + recv[f, way, 0].astype(F32)).astype(BF16)
            summed.start()
        for f in range(2):
            p = position(axes[f][level])
            both = [entry for entry in plan if entry[0] == f]
            for h in range(2):
                both[1 - h][4].wait_recv()
                both[h][5].wait_recv()
                total = (
                    chunk(f, p, h)[...].astype(F32)
                    + recv[f, h, 2].astype(F32)
                    + recv[f, 1 - h, 1].astype(F32)
                )
                store(f, h, total)
        for f, way, near, first, plain, summed in plan:
            first.wait_send()
            plain.wait_send()
            summed.wait_send()

    def store_a(f, h, total):
        kept[f, :, h] = total.astype(BF16)

    def store_b(f, h, total):
        last[f, h] = total
        last_half[f, h] = total.astype(BF16)

    stage(0, chunk_a, ra, acc_a, sa, qa, store_a)
    stage(1, chunk_b, rb, acc_b, sb, qb, store_b)
    swaps = [
        remote(last_half.at[f, 1 - me.zh], rc.at[f], sc.at[f], qc.at[f], me.across()) for f in range(2)
    ]
    for swap in swaps:
        swap.start()
    sums = []
    for f, swap in enumerate(swaps):
        swap.wait_recv()
        sums.append(last[f, me.zh] + rc[f].astype(F32))
    for swap in swaps:
        swap.wait_send()
    return sums


def reduce_scratch():
    dma = pltpu.SemaphoreType.DMA
    bufs = [
        pltpu.VMEM((2, 2, 3, 4, 16, HALF), BF16),
        pltpu.VMEM((2, 2, 4, 16, HALF), BF16),
        pltpu.VMEM((2, 2, 3, 16, HALF), BF16),
        pltpu.VMEM((2, 2, 16, HALF), BF16),
        pltpu.VMEM((2, 4, 2, 16, HALF), BF16),
        pltpu.VMEM((2, 2, 16, HALF), F32),
        pltpu.VMEM((2, 2, 16, HALF), BF16),
        pltpu.VMEM((2, 16, HALF), BF16),
    ]
    sems = [dma((2, 2, 3)), dma((2, 2, 3)), dma((2, 2, 3)), dma((2, 2, 3)), dma((2,)), dma((2,))]
    return bufs, sems


def meet(me, pairs):
    barrier = pltpu.get_barrier_semaphore()
    around = [me.near("x", 1), me.near("x", -1), me.near("y", 1), me.near("y", -1), me.across()]
    if pairs:
        around += [(me.z_pair, me.t), (me.core_pair, me.t)]
    for device in around:
        greet(barrier, device)
    pl.semaphore_wait(barrier, len(around))


def middle_kernel(share, hidden, gain, upq, dnq, gathered, middle, up, down, *scratch):
    bufs, sems = scratch[:8], scratch[8:14]
    (field, rows, h_sem, z_s, z_r, c_s, c_r, p_s, p_r, own_sem, a_s, a_r, b_s, b_r, x_s, x_r, o_sem) = scratch[14:]
    me = Place()
    take = pltpu.make_async_copy(hidden.at[pl.ds(pl.multiple_of(me.t * 16, 16), 16), :], rows, h_sem)
    take.start()
    meet(me, True)

    def place(full, apart, flip_z, flip_c):
        zl = (me.zl + apart + flip_z) % 2
        core = (me.core + flip_c) % 2
        return full.at[zl * 2 + core, :, (me.zh + apart) % 2]

    moves = []
    for k, (quarter, full) in enumerate(((upq, up), (dnq, down))):
        for apart in range(2):
            n = 2 * k + apart
            src = quarter.at[pl.ds(4 * apart, 4)]
            dst = place(full, apart, 0, 0)
            to_z = remote(src, dst, z_s.at[n], z_r.at[n], (me.z_pair, me.t))
            to_c = remote(src, dst, c_s.at[n], c_r.at[n], (me.core_pair, me.t))
            own = pltpu.make_async_copy(src, dst, own_sem.at[n])
            came = place(full, apart, 1, 0)
            passed = remote(came, came, p_s.at[n], p_r.at[n], (me.core_pair, me.t))
            moves.append((to_z, to_c, own, passed))
    for to_z, to_c, own, passed in moves:
        to_z.start()
        to_c.start()
        own.start()

    left, right = reduce_rows(me, share, bufs, sems)
    take.wait()
    mid_l = (rows[:, :HALF].astype(F32) + left).astype(BF16)
    mid_r = (rows[:, HALF:].astype(F32) + right).astype(BF16)
    middle[:, :HALF] = mid_l
    middle[:, HALF:] = mid_r
    values = middle[...].astype(F32)
    center = values - jnp.mean(values, axis=-1, keepdims=True)
    spread = jnp.mean(center * center, axis=-1, keepdims=True)
    field[me.x, me.zh, me.y] = (center * lax.rsqrt(spread + EPSILON) * gain[...]).astype(BF16)

    swap = remote(
        field.at[me.x, me.zh, me.y], field.at[me.x, me.zh, me.y], x_s, x_r, me.across()
    )
    swap.start()
    swap.wait_recv()

    def view_b(f, q, h):
        cols = pl.ds(f * HALF, HALF)
        lane = slice(None) if h is None else h
        if f == 0:
            return field.at[me.x, lane, q, :, cols]
        return field.at[q, lane, me.y, :, cols]

    def view_a(f, q, h):
        cols = pl.ds(f * HALF, HALF)
        lane = slice(None) if h is None else h
        if f == 0:
            return field.at[q, lane, :, :, cols]
        return field.at[:, lane, q, :, cols]

    def spread_out(view, axes, s_sem, r_sem):
        plan = []
        for f in range(2):
            axis = axes[f]
            p = me.x if axis == "x" else me.y
            for way in range(2):
                delta = 1 - 2 * way
                device = me.near(axis, delta)
                unit = view(f, p, None)
                came = view(f, (p + 4 - delta) % 4, way)
                plan.append(
                    (
                        remote(unit, unit, s_sem.at[f, way, 0], r_sem.at[f, way, 0], device),
                        remote(came, came, s_sem.at[f, way, 1], r_sem.at[f, way, 1], device),
                    )
                )
        for whole, half in plan:
            whole.start()
        for whole, half in plan:
            whole.wait_recv()
            half.start()
        for whole, half in plan:
            half.wait_recv()
        for whole, half in plan:
            whole.wait_send()
            half.wait_send()

    spread_out(view_b, ("y", "x"), b_s, b_r)
    for to_z, to_c, own, passed in moves[:2]:
        to_z.wait_recv()
        passed.start()
    spread_out(view_a, ("x", "y"), a_s, a_r)
    write = pltpu.make_async_copy(field, gathered, o_sem)
    write.start()
    for to_z, to_c, own, passed in moves[2:]:
        to_z.wait_recv()
        passed.start()
    swap.wait_send()
    for to_z, to_c, own, passed in moves:
        to_c.wait_recv()
        passed.wait_recv()
        own.wait()
        to_z.wait_send()
        to_c.wait_send()
        passed.wait_send()
    write.wait()


def middle_step(share, hidden, gain, upq, dnq):
    dma = pltpu.SemaphoreType.DMA
    bufs, sems = reduce_scratch()
    any_spec = pl.BlockSpec(memory_space=pl.ANY)
    vmem = pl.BlockSpec(memory_space=pltpu.VMEM)
    return pl.pallas_call(
        middle_kernel,
        out_shape=(
            jax.ShapeDtypeStruct((4, 2, 4, 16, D), BF16),
            jax.ShapeDtypeStruct((16, D), BF16),
            jax.ShapeDtypeStruct((4, 4, 2, 128, 512), BF16),
            jax.ShapeDtypeStruct((4, 4, 2, 128, 512), BF16),
        ),
        in_specs=[vmem, any_spec, vmem, any_spec, any_spec],
        out_specs=[any_spec, vmem, any_spec, any_spec],
        scratch_shapes=bufs
        + sems
        + [pltpu.VMEM((4, 2, 4, 16, D), BF16), pltpu.VMEM((16, D), BF16), dma(())]
        + [dma((4,))] * 7
        + [dma((2, 2, 2))] * 4
        + [dma(()), dma(()), dma(())],
        compiler_params=pltpu.CompilerParams(
            collective_id=1, has_side_effects=True, vmem_limit_bytes=48 << 20
        ),
        name="middle",
    )(share.reshape(4, 2, 4, 16, D), hidden, gain.reshape(1, D), upq, dnq)


def last_kernel(share, middle, result, *scratch):
    bufs, sems = scratch[:8], scratch[8:14]
    me = Place()
    meet(me, False)
    left, right = reduce_rows(me, share, bufs, sems)
    result[:, :HALF] = (middle[:, :HALF].astype(F32) + left).astype(BF16)
    result[:, HALF:] = (middle[:, HALF:].astype(F32) + right).astype(BF16)


def last_step(share, middle):
    bufs, sems = reduce_scratch()
    vmem = pl.BlockSpec(memory_space=pltpu.VMEM)
    return pl.pallas_call(
        last_kernel,
        out_shape=jax.ShapeDtypeStruct((16, D), BF16),
        in_specs=[vmem, vmem],
        out_specs=vmem,
        scratch_shapes=bufs + sems,
        compiler_params=pltpu.CompilerParams(
            collective_id=2, has_side_effects=True, vmem_limit_bytes=48 << 20
        ),
        name="last",
    )(share.reshape(4, 2, 4, 16, D), middle)


def shards(
    hidden, segment_ids, first_gain, second_gain, qkv_master, out_master, up_master, down_master
):
    qo, upq, dnq = relay(qkv_master.transpose(1, 0, 2), out_master.T, up_master, down_master.T)
    qo = qo.reshape(4, D, HD)
    qkv = qo[:3]
    out_t = qo[3]
    normed = layer_norm(hidden, first_gain).astype(BF16)
    projected = jnp.einsum("nd,kdc->knc", normed, qkv, preferred_element_type=F32).astype(BF16)
    queries, key_rows, value_rows = projected[0], projected[1], projected[2]
    length = hidden.shape[0]
    slope = jnp.exp2(-8.0 * (lax.axis_index("tensor").astype(F32) + 1.0) / (D // HD))
    position = jnp.arange(length)
    distance = (position[:, None] - position[None, :]).astype(F32)
    allowed = (segment_ids[:, None] == segment_ids[None, :]) & (distance >= 0)
    scores = lax.dot_general(
        queries, key_rows, (((1,), (1,)), ((), ())), preferred_element_type=F32
    ) / math.sqrt(HD)
    scores = jnp.where(allowed, scores - slope * distance, -jnp.inf)
    highest = jnp.max(scores, axis=-1, keepdims=True)
    raised = jnp.exp(scores - highest)
    weights = (raised / jnp.sum(raised, axis=-1, keepdims=True)).astype(BF16)
    context = jnp.dot(weights, value_rows, preferred_element_type=F32).astype(BF16)
    share = lax.dot_general(
        context, out_t, (((1,), (1,)), ((), ())), preferred_element_type=F32
    ).astype(BF16)
    gathered, middle, up, down = middle_step(share, hidden, second_gain, upq, dnq)
    up = up.reshape(D, 512)
    down_t = down.reshape(D, 512)
    activated = jax.nn.gelu(
        jnp.dot(gathered.reshape(512, D), up, preferred_element_type=F32), approximate=False
    ).astype(BF16)
    share_two = lax.dot_general(
        activated, down_t, (((1,), (1,)), ((), ())), preferred_element_type=F32
    ).astype(BF16)
    new_hidden = last_step(share_two, middle)
    return (
        new_hidden,
        key_rows,
        value_rows,
        qkv.transpose(1, 0, 2),
        out_t.T,
        up,
        down_t.T,
    )


def solution(mesh):
    in_specs = (
        P("dp", None),
        P("dp"),
        P(),
        P(),
        P(("dp", "tensor"), None, None),
        P(None, ("dp", "tensor")),
        P(("dp", "tensor"), None),
        P(None, ("dp", "tensor")),
    )
    out_specs = (
        P(("dp", "tensor"), None),
        P("dp", "tensor"),
        P("dp", "tensor"),
        P(None, None, "tensor"),
        P("tensor", None),
        P(None, "tensor"),
        P("tensor", None),
    )
    return jax.shard_map(shards, mesh=mesh, in_specs=in_specs, out_specs=out_specs, check_vma=False)
```

```python
import math

import jax
import jax.numpy as jnp
from jax import lax
from jax.experimental import pallas as pl
from jax.experimental.pallas import tpu as pltpu
from jax.sharding import PartitionSpec as P

D = 4096
HD = 128
EPSILON = 1e-05
MESH = pl.DeviceIdType.MESH
BF16 = jnp.bfloat16
F32 = jnp.float32


class Place:
    def __init__(self):
        self.dp = lax.axis_index("dp")
        self.t = lax.axis_index("tensor")
        self.zl = self.dp // 2
        self.core = self.dp % 2
        self.x = self.t // 8
        self.zh = (self.t // 4) % 2
        self.y = self.t % 4
        self.z_pair = (1 - self.zl) * 2 + self.core
        self.core_pair = self.zl * 2 + (1 - self.core)

    def near(self, axis, delta):
        if axis == "x":
            return (self.dp, ((self.x + delta) % 4) * 8 + self.zh * 4 + self.y)
        return (self.dp, self.x * 8 + self.zh * 4 + (self.y + delta) % 4)

    def across(self):
        return (self.dp, self.x * 8 + (1 - self.zh) * 4 + self.y)


def remote(src, dst, send_sem, recv_sem, device):
    return pltpu.make_async_remote_copy(
        src_ref=src,
        dst_ref=dst,
        send_sem=send_sem,
        recv_sem=recv_sem,
        device_id=device,
        device_id_type=MESH,
    )


def greet(barrier, device):
    pl.semaphore_signal(barrier, inc=1, device_id=device, device_id_type=MESH)


HALF = 2048


def reduce_rows(me, share, bufs, sems, between):
    ra, acc_a, rb, acc_b, kept, last, last_half, rc = bufs
    sa, qa, sb, qb, sc, qc = sems
    axes = (("x", "y"), ("y", "x"))

    def chunk_a(f, q, h):
        if f == 0:
            return share.at[q, h, :, :, pl.ds(0, HALF)]
        return share.at[:, h, q, :, pl.ds(HALF, HALF)]

    def chunk_b(f, q, h):
        return kept.at[f, q, h]

    def position(axis):
        return me.x if axis == "x" else me.y

    def stage(level, chunk, recv, acc, s_sem, r_sem, store):
        started = []
        plan = []
        for f in range(2):
            axis = axes[f][level]
            p = position(axis)
            far = (p + 2) % 4
            for way in range(2):
                delta = 1 - 2 * way
                near = (p + delta) % 4
                device = me.near(axis, delta)
                first = remote(
                    chunk(f, far, way), recv.at[f, way, 0], s_sem.at[f, way, 0], r_sem.at[f, way, 0], device
                )
                plain = remote(
                    chunk(f, near, 1 - way), recv.at[f, way, 1], s_sem.at[f, way, 1], r_sem.at[f, way, 1], device
                )
                summed = remote(
                    acc.at[f, way], recv.at[f, way, 2], s_sem.at[f, way, 2], r_sem.at[f, way, 2], device
                )
                plan.append((f, way, near, first, plain, summed))
        for f, way, near, first, plain, summed in plan:
            first.start()
        for f, way, near, first, plain, summed in plan:
            plain.start()
        for f, way, near, first, plain, summed in plan:
            first.wait_recv()
            acc[f, way] = (chunk(f, near, way)[...].astype(F32) + recv[f, way, 0].astype(F32)).astype(BF16)
            summed.start()
        for f in range(2):
            p = position(axes[f][level])
            both = [entry for entry in plan if entry[0] == f]
            for h in range(2):
                both[1 - h][4].wait_recv()
                both[h][5].wait_recv()
                total = (
                    chunk(f, p, h)[...].astype(F32)
                    + recv[f, h, 2].astype(F32)
                    + recv[f, 1 - h, 1].astype(F32)
                )
                store(f, h, total)
        for f, way, near, first, plain, summed in plan:
            first.wait_send()
            plain.wait_send()
            summed.wait_send()

    def store_a(f, h, total):
        kept[f, :, h] = total.astype(BF16)

    def store_b(f, h, total):
        last[f, h] = total
        last_half[f, h] = total.astype(BF16)

    stage(0, chunk_a, ra, acc_a, sa, qa, store_a)
    between()
    stage(1, chunk_b, rb, acc_b, sb, qb, store_b)
    swaps = [
        remote(last_half.at[f, 1 - me.zh], rc.at[f], sc.at[f], qc.at[f], me.across()) for f in range(2)
    ]
    for swap in swaps:
        swap.start()
    sums = []
    for f, swap in enumerate(swaps):
        swap.wait_recv()
        sums.append(last[f, me.zh] + rc[f].astype(F32))
    for swap in swaps:
        swap.wait_send()
    return sums


def reduce_scratch():
    dma = pltpu.SemaphoreType.DMA
    bufs = [
        pltpu.VMEM((2, 2, 3, 4, 16, HALF), BF16),
        pltpu.VMEM((2, 2, 4, 16, HALF), BF16),
        pltpu.VMEM((2, 2, 3, 16, HALF), BF16),
        pltpu.VMEM((2, 2, 16, HALF), BF16),
        pltpu.VMEM((2, 4, 2, 16, HALF), BF16),
        pltpu.VMEM((2, 2, 16, HALF), F32),
        pltpu.VMEM((2, 2, 16, HALF), BF16),
        pltpu.VMEM((2, 16, HALF), BF16),
    ]
    sems = [dma((2, 2, 3)), dma((2, 2, 3)), dma((2, 2, 3)), dma((2, 2, 3)), dma((2,)), dma((2,))]
    return bufs, sems


class Relay:
    def __init__(self, me, source, wide, stage, sems):
        self.me, self.source, self.wide, self.stage = me, source, wide, stage
        self.s, self.own, self.r, self.zs, self.zr, self.cs, self.cr, self.ps, self.pr = sems

    def holder(self, step):
        me = self.me
        other = (me.t + step) % 32
        apart = (me.zh + (other // 4) % 2) % 2
        return other, apart, ((me.zl + apart) % 2) * 2 + me.core

    def group(self, slot, flip_z, flip_c):
        me = self.me
        apart = slot // 4
        zl = (me.zl + apart + flip_z) % 2
        core = (me.core + flip_c) % 2
        return (zl * 2 + core) * 8 + (slot % 4) * 2 + (me.zh + apart) % 2

    def at(self, group, rows=None):
        lead = (slice(None),) * (len(self.stage.shape) - 3)
        if rows is None:
            return self.stage.at[lead + (group,)]
        return self.stage.at[lead + (group, rows)]

    def cut(self, other):
        lead = (slice(None),) * (len(self.source.shape) - 1)
        return self.source.at[lead + (pl.ds(pl.multiple_of(other * self.wide, self.wide), self.wide),)]

    def own_piece(self):
        me = self.me
        mine = me.dp * 8 + me.x * 2 + me.zh
        return self.at(mine, pl.ds(pl.multiple_of(me.y * 32, 32), 32))

    def send(self):
        me = self.me

        def body(step, carry):
            other, apart, group = self.holder(step)
            remote(
                self.cut(other), self.own_piece(), self.s, self.r.at[apart * 4 + me.x], (group, other)
            ).start()
            return carry

        lax.fori_loop(1, 32, body, 0)
        pltpu.make_async_copy(self.cut(me.t), self.own_piece(), self.own).start()

    def settle(self):
        pltpu.make_async_copy(self.cut(self.me.t), self.own_piece(), self.own).wait()

    def wait_slot(self, slot):
        me = self.me
        group = self.group(slot, 0, 0)

        def got(count):
            ref = self.at(group, pl.ds(0, count))
            remote(ref, ref, self.s, self.r.at[slot], (me.core_pair, me.t)).wait_recv()

        @pl.when(slot != me.x)
        def _():
            got(128)

        @pl.when(slot == me.x)
        def _():
            got(96)

    def to_z(self, slot):
        ref = self.at(self.group(slot, 0, 0))
        return remote(ref, ref, self.zs.at[slot], self.zr.at[slot], (self.me.z_pair, self.me.t))

    def to_core(self, slot):
        ref = self.at(self.group(slot, 0, 0))
        return remote(ref, ref, self.cs.at[slot], self.cr.at[slot], (self.me.core_pair, self.me.t))

    def pass_on(self, slot):
        ref = self.at(self.group(slot, 1, 0))
        return remote(ref, ref, self.ps.at[slot], self.pr.at[slot], (self.me.core_pair, self.me.t))

    def got(self, slot, flip_z, flip_c, sem):
        ref = self.at(self.group(slot, flip_z, flip_c))
        remote(ref, ref, self.s, sem, (self.me.core_pair, self.me.t)).wait_recv()

    def forward(self, first, last):
        def body(slot, carry):
            self.wait_slot(slot)
            self.to_z(slot).start()
            self.to_core(slot).start()
            return carry

        lax.fori_loop(first, last, body, 0)

    def relay_on(self, first, last):
        def body(slot, carry):
            self.got(slot, 1, 0, self.zr.at[slot])
            self.pass_on(slot).start()
            return carry

        lax.fori_loop(first, last, body, 0)

    def complete(self):
        def body(slot, carry):
            self.got(slot, 0, 1, self.cr.at[slot])
            self.got(slot, 1, 1, self.pr.at[slot])
            return carry

        lax.fori_loop(0, 8, body, 0)

    def drain(self):
        def body(slot, carry):
            self.to_z(slot).wait_send()
            self.to_core(slot).wait_send()
            self.pass_on(slot).wait_send()
            return carry

        lax.fori_loop(0, 8, body, 0)
        lead = (slice(None),) * (len(self.source.shape) - 1)
        sent = self.source.at[lead + (pl.ds(0, 31 * self.wide),)]
        remote(sent, sent, self.s, self.s, (self.me.core_pair, self.me.t)).wait_send()


def norm_rows(values, gain):
    center = values - jnp.mean(values, axis=-1, keepdims=True)
    spread = jnp.mean(center * center, axis=-1, keepdims=True)
    return (center * lax.rsqrt(spread + EPSILON) * gain).astype(BF16)


def gather_rows(me, field, view, axes, s_sem, r_sem, between):
    plan = []
    for f in range(2):
        axis = axes[f]
        p = me.x if axis == "x" else me.y
        for way in range(2):
            delta = 1 - 2 * way
            device = me.near(axis, delta)
            unit = view(f, p, None)
            came = view(f, (p + 4 - delta) % 4, way)
            plan.append(
                (
                    remote(unit, unit, s_sem.at[f, way, 0], r_sem.at[f, way, 0], device),
                    remote(came, came, s_sem.at[f, way, 1], r_sem.at[f, way, 1], device),
                )
            )
    for whole, half in plan:
        whole.start()
    between()
    for whole, half in plan:
        whole.wait_recv()
        half.start()
    for whole, half in plan:
        half.wait_recv()
    for whole, half in plan:
        whole.wait_send()
        half.wait_send()


def attend(queries, keys, values, seg_col, seg_row, slope, context):
    scale = 1.0 / math.sqrt(HD)
    for block in range(4):
        rows = pl.ds(block * 128, 128)
        reach = (block + 1) * 128
        cols = pl.ds(0, reach)
        scores = (
            lax.dot_general(
                queries[rows, :], keys[cols, :], (((1,), (1,)), ((), ())), preferred_element_type=F32
            )
            * scale
        )
        n = lax.broadcasted_iota(jnp.int32, (128, reach), 0) + block * 128
        p = lax.broadcasted_iota(jnp.int32, (128, reach), 1)
        scores = scores - slope * (n - p).astype(F32)
        allowed = (seg_col[rows, :] == seg_row[:, cols]) & (p <= n)
        scores = jnp.where(allowed, scores, -jnp.inf)
        highest = jnp.max(scores, axis=-1, keepdims=True)
        raised = jnp.exp(scores - highest)
        weights = (raised / jnp.sum(raised, axis=-1, keepdims=True)).astype(BF16)
        context[rows, :] = jnp.dot(weights, values[cols, :], preferred_element_type=F32).astype(BF16)


def layer_kernel(*refs):
    (hidden, seg_col, seg_row, slope, gain_one, gain_two, q_in, o_in, u_in, w_in) = refs[:10]
    (new_hidden, key_out, value_out, qkv_out, out_out, up_out, down_out) = refs[10:17]
    rest = refs[17:]
    (q_f, o_f, u_f, w_f, h_v, sq, su, sw, qo, up, down, normed, field, share, acc, q_v, k_v, v_v, ctx, act, middle, result) = rest[:22]
    in_sem, out_sem = rest[22:24]
    relay_sems = [rest[24 + 9 * k : 33 + 9 * k] for k in range(3)]
    rest = rest[51:]
    bufs_one, sems_one, bufs_two, sems_two = rest[:8], rest[8:14], rest[14:22], rest[22:28]
    a_s, a_r, b_s, b_r, x_s, x_r = rest[28:]
    me = Place()

    loads = [
        pltpu.make_async_copy(src, dst, in_sem.at[k])
        for k, (src, dst) in enumerate(
            ((q_in, q_f), (o_in, o_f), (u_in, u_f), (w_in, w_f), (hidden, h_v))
        )
    ]
    for load in loads:
        load.start()
    r_q = Relay(me, sq, 128, qo, relay_sems[0])
    r_u = Relay(me, su, 512, up, relay_sems[1])
    r_d = Relay(me, sw, 512, down, relay_sems[2])

    barrier = pltpu.get_barrier_semaphore()

    def hello(step, carry):
        other, _, group = r_q.holder(step)
        greet(barrier, (group, other))
        return carry

    lax.fori_loop(1, 32, hello, 0)
    greet(barrier, (me.z_pair, me.t))
    greet(barrier, (me.core_pair, me.t))
    greet(barrier, me.across())
    loads[0].wait()
    loads[1].wait()
    sq[0:3] = q_f[...].astype(BF16)
    sq[3] = o_f[...].astype(BF16)
    pl.semaphore_wait(barrier, 34)
    r_q.send()

    loads[4].wait()
    r_q.settle()

    def opening(slot, carry):
        @pl.loop(0, 2)
        def _(part):
            rows = pl.ds(pl.multiple_of(slot * 64 + part * 32, 32), 32)
            normed[rows, :] = norm_rows(h_v[rows, :].astype(F32), gain_one[...])

        r_q.wait_slot(slot)
        r_q.to_z(slot).start()
        r_q.to_core(slot).start()
        return carry

    lax.fori_loop(0, 8, opening, 0)

    loads[2].wait()
    loads[3].wait()

    @pl.loop(0, 4)
    def _(part):
        cols = pl.ds(pl.multiple_of(part * 4096, 4096), 4096)
        su[:, cols] = u_f[:, cols].astype(BF16)

    r_u.send()

    @pl.loop(0, 4)
    def _(part):
        cols = pl.ds(pl.multiple_of(part * 4096, 4096), 4096)
        sw[:, cols] = w_f[:, cols].astype(BF16)

    r_d.send()
    r_q.relay_on(0, 8)
    r_u.settle()
    r_d.settle()
    r_u.forward(0, 8)
    r_q.complete()
    save_q = pltpu.make_async_copy(qo.at[pl.ds(0, 3)], qkv_out, out_sem.at[0])
    save_o = pltpu.make_async_copy(qo.at[3], out_out, out_sem.at[1])
    save_q.start()
    save_o.start()

    acc_q = acc.at[:, pl.ds(0, 384)]
    for part in range(8):
        cols = pl.ds(part * 512, 512)
        block = jnp.concatenate(
            [qo[k, part * 4 : part * 4 + 4].reshape(512, 128) for k in range(3)], axis=1
        )
        product = jnp.dot(normed[:, cols], block, preferred_element_type=F32)
        if part == 0:
            acc_q[...] = product
        else:
            acc_q[...] += product
    q_v[...] = acc[:, 0:128].astype(BF16)
    k_v[...] = acc[:, 128:256].astype(BF16)
    v_v[...] = acc[:, 256:384].astype(BF16)
    save_k = pltpu.make_async_copy(k_v, key_out, out_sem.at[2])
    save_v = pltpu.make_async_copy(v_v, value_out, out_sem.at[3])
    save_k.start()
    save_v.start()
    attend(q_v, k_v, v_v, seg_col, seg_row, slope[0:1, 0:1], ctx)

    @pl.loop(0, 8)
    def _(part):
        block = qo[3, pl.ds(part * 4, 4)].reshape(512, 128)
        product = lax.dot_general(
            ctx[...], block, (((1,), (1,)), ((), ())), preferred_element_type=F32
        ).astype(BF16)
        cols = pl.ds(pl.multiple_of(part * 512, 512), 512)
        share[:, :, :, :, cols] = product.reshape(4, 2, 4, 16, 512)

    def after_first():
        r_u.relay_on(0, 8)
        r_d.forward(0, 4)

    left, right = reduce_rows(me, share, bufs_one, sems_one, after_first)
    own_rows = pl.ds(pl.multiple_of(me.t * 16, 16), 16)
    middle[:, :HALF] = (h_v[own_rows, :HALF].astype(F32) + left).astype(BF16)
    middle[:, HALF:] = (h_v[own_rows, HALF:].astype(F32) + right).astype(BF16)
    field[me.x, me.zh, me.y] = norm_rows(middle[...].astype(F32), gain_two[...])

    spot = field.at[me.x, me.zh, me.y]
    swap = remote(spot, spot, x_s, x_r, me.across())
    swap.start()
    swap.wait_recv()
    swap.wait_send()

    def view_b(f, q, h):
        cols = pl.ds(f * HALF, HALF)
        lane = slice(None) if h is None else h
        if f == 0:
            return field.at[me.x, lane, q, :, cols]
        return field.at[q, lane, me.y, :, cols]

    def view_a(f, q, h):
        cols = pl.ds(f * HALF, HALF)
        lane = slice(None) if h is None else h
        if f == 0:
            return field.at[q, lane, :, :, cols]
        return field.at[:, lane, q, :, cols]

    def rest_of_down():
        r_d.forward(4, 8)
        r_d.relay_on(0, 4)

    gather_rows(me, field, view_b, ("y", "x"), b_s, b_r, rest_of_down)
    gather_rows(me, field, view_a, ("x", "y"), a_s, a_r, lambda: None)
    r_u.complete()
    save_u = pltpu.make_async_copy(up, up_out, out_sem.at[4])
    save_u.start()
    r_d.relay_on(4, 8)

    for part in range(8):
        rows = field[:, :, :, :, part * 512 : part * 512 + 512].reshape(512, 512)
        block = up[part * 4 : part * 4 + 4].reshape(512, 512)
        product = jnp.dot(rows, block, preferred_element_type=F32)
        if part == 0:
            acc[...] = product
        else:
            acc[...] += product

    @pl.loop(0, 8)
    def _(part):
        rows = pl.ds(pl.multiple_of(part * 64, 64), 64)
        values = acc[rows, :]
        act[rows, :] = (0.5 * values * (1.0 + lax.erf(values * math.sqrt(0.5)))).astype(BF16)

    r_d.complete()
    save_d = pltpu.make_async_copy(down, down_out, out_sem.at[5])
    save_d.start()

    @pl.loop(0, 8)
    def _(part):
        block = down[pl.ds(part * 4, 4)].reshape(512, 512)
        product = lax.dot_general(
            act[...], block, (((1,), (1,)), ((), ())), preferred_element_type=F32
        ).astype(BF16)
        cols = pl.ds(pl.multiple_of(part * 512, 512), 512)
        share[:, :, :, :, cols] = product.reshape(4, 2, 4, 16, 512)

    left, right = reduce_rows(me, share, bufs_two, sems_two, lambda: None)
    result[:, :HALF] = (middle[:, :HALF].astype(F32) + left).astype(BF16)
    result[:, HALF:] = (middle[:, HALF:].astype(F32) + right).astype(BF16)
    save_n = pltpu.make_async_copy(result, new_hidden, out_sem.at[6])
    save_n.start()
    for relay in (r_q, r_u, r_d):
        relay.drain()
    for save in (save_q, save_o, save_k, save_v, save_u, save_d, save_n):
        save.wait()


def layer(hidden, seg, slope, gain_one, gain_two, qkv, out, up, down):
    any_spec = pl.BlockSpec(memory_space=pl.ANY)
    vmem = pl.BlockSpec(memory_space=pltpu.VMEM)
    dma = pltpu.SemaphoreType.DMA
    bufs_one, sems_one = reduce_scratch()
    bufs_two, sems_two = reduce_scratch()
    relay_sems = [dma(()), dma(())] + [dma((8,))] * 7
    return pl.pallas_call(
        layer_kernel,
        out_shape=(
            jax.ShapeDtypeStruct((16, D), BF16),
            jax.ShapeDtypeStruct((512, HD), BF16),
            jax.ShapeDtypeStruct((512, HD), BF16),
            jax.ShapeDtypeStruct((3, 32, 128, HD), BF16),
            jax.ShapeDtypeStruct((32, 128, HD), BF16),
            jax.ShapeDtypeStruct((32, 128, 512), BF16),
            jax.ShapeDtypeStruct((32, 128, 512), BF16),
        ),
        in_specs=[any_spec, vmem, vmem, vmem, vmem, vmem] + [any_spec] * 4,
        out_specs=[any_spec] * 7,
        scratch_shapes=[
            pltpu.VMEM((3, 32, 4096), F32),
            pltpu.VMEM((32, 4096), F32),
            pltpu.VMEM((32, 16384), F32),
            pltpu.VMEM((32, 16384), F32),
            pltpu.VMEM((512, D), BF16),
            pltpu.VMEM((4, 32, 4096), BF16),
            pltpu.VMEM((32, 16384), BF16),
            pltpu.VMEM((32, 16384), BF16),
            pltpu.VMEM((4, 32, 128, 128), BF16),
            pltpu.VMEM((32, 128, 512), BF16),
            pltpu.VMEM((32, 128, 512), BF16),
            pltpu.VMEM((512, D), BF16),
            pltpu.VMEM((4, 2, 4, 16, D), BF16),
            pltpu.VMEM((4, 2, 4, 16, D), BF16),
            pltpu.VMEM((512, 512), F32),
            pltpu.VMEM((512, HD), BF16),
            pltpu.VMEM((512, HD), BF16),
            pltpu.VMEM((512, HD), BF16),
            pltpu.VMEM((512, HD), BF16),
            pltpu.VMEM((512, 512), BF16),
            pltpu.VMEM((16, D), BF16),
            pltpu.VMEM((16, D), BF16),
            dma((5,)),
            dma((7,)),
        ]
        + relay_sems * 3
        + bufs_one
        + sems_one
        + bufs_two
        + sems_two
        + [dma((2, 2, 2))] * 4
        + [dma(()), dma(())],
        compiler_params=pltpu.CompilerParams(
            collective_id=0, has_side_effects=True, vmem_limit_bytes=62 << 20
        ),
        name="layer",
    )(hidden, seg.reshape(512, 1), seg.reshape(1, 512), slope, gain_one, gain_two, qkv, out, up, down)


def shards(
    hidden, segment_ids, first_gain, second_gain, qkv_master, out_master, up_master, down_master
):
    slope = jnp.exp2(-8.0 * (lax.axis_index("tensor").astype(F32) + 1.0) / (D // HD))
    new_hidden, keys, values, qkv, out_t, up, down_t = layer(
        hidden,
        segment_ids,
        jnp.full((1, 128), slope, F32),
        first_gain.reshape(1, D),
        second_gain.reshape(1, D),
        qkv_master.transpose(1, 0, 2),
        out_master.T,
        up_master,
        down_master.T,
    )
    return (
        new_hidden,
        keys,
        values,
        qkv.reshape(3, D, HD).transpose(1, 0, 2),
        out_t.reshape(D, HD).T,
        up.reshape(D, 512),
        down_t.reshape(D, 512).T,
    )


def solution(mesh):
    in_specs = (
        P("dp", None),
        P("dp"),
        P(),
        P(),
        P(("dp", "tensor"), None, None),
        P(None, ("dp", "tensor")),
        P(("dp", "tensor"), None),
        P(None, ("dp", "tensor")),
    )
    out_specs = (
        P(("dp", "tensor"), None),
        P("dp", "tensor"),
        P("dp", "tensor"),
        P(None, None, "tensor"),
        P("tensor", None),
        P(None, "tensor"),
        P("tensor", None),
    )
    return jax.shard_map(shards, mesh=mesh, in_specs=in_specs, out_specs=out_specs, check_vma=False)
```

```python
import math

import jax
import jax.numpy as jnp
from jax import lax
from jax.experimental import pallas as pl
from jax.experimental.pallas import tpu as pltpu
from jax.sharding import PartitionSpec as P

D = 4096
HD = 128
EPSILON = 1e-05
MESH = pl.DeviceIdType.MESH
BF16 = jnp.bfloat16
F32 = jnp.float32


class Place:
    def __init__(self):
        self.dp = lax.axis_index("dp")
        self.t = lax.axis_index("tensor")
        self.zl = self.dp // 2
        self.core = self.dp % 2
        self.x = self.t // 8
        self.zh = (self.t // 4) % 2
        self.y = self.t % 4
        self.z_pair = (1 - self.zl) * 2 + self.core
        self.core_pair = self.zl * 2 + (1 - self.core)

    def near(self, axis, delta):
        if axis == "x":
            return (self.dp, ((self.x + delta) % 4) * 8 + self.zh * 4 + self.y)
        return (self.dp, self.x * 8 + self.zh * 4 + (self.y + delta) % 4)

    def across(self):
        return (self.dp, self.x * 8 + (1 - self.zh) * 4 + self.y)


def remote(src, dst, send_sem, recv_sem, device):
    return pltpu.make_async_remote_copy(
        src_ref=src,
        dst_ref=dst,
        send_sem=send_sem,
        recv_sem=recv_sem,
        device_id=device,
        device_id_type=MESH,
    )


def greet(barrier, device):
    pl.semaphore_signal(barrier, inc=1, device_id=device, device_id_type=MESH)


HALF = 2048
PART = 1024


def reduce_rows(me, share, bufs, sems, while_first, while_second, pump=lambda count: None):
    ra, acc_a, rb, acc_b, kept, last, last_half, rc = bufs
    sa, qa, sb, qb, sc, qc = sems
    axes = (("x", "y"), ("y", "x"))

    def chunk_a(f, s, q, h):
        cols = pl.ds(f * HALF + s * PART, PART)
        if f == 0:
            return share.at[q, h, :, :, cols]
        return share.at[:, h, q, :, cols]

    def chunk_b(f, s, q, h):
        return kept.at[f, s, q, h]

    def position(f, level):
        return me.x if axes[f][level] == "x" else me.y

    class Ring:
        def __init__(self, level, s, chunk, recv, acc, s_sem, r_sem):
            self.level, self.s, self.chunk, self.recv, self.acc = level, s, chunk, recv, acc
            self.plan = []
            for f in range(2):
                p = position(f, level)
                far = (p + 2) % 4
                for way in range(2):
                    delta = 1 - 2 * way
                    near = (p + delta) % 4
                    device = me.near(axes[f][level], delta)
                    copies = [
                        remote(src, recv.at[f, s, way, k], s_sem.at[f, s, way, k], r_sem.at[f, s, way, k], device)
                        for k, src in enumerate(
                            (chunk(f, s, far, way), chunk(f, s, near, 1 - way), acc.at[f, s, way])
                        )
                    ]
                    self.plan.append((f, way, near, copies))

        def start(self, k):
            for f, way, near, copies in self.plan:
                copies[k].start()

        def accumulate(self):
            s = self.s
            for f, way, near, copies in self.plan:
                copies[0].wait_recv()
                self.acc[f, s, way] = (
                    self.chunk(f, s, near, way)[...].astype(F32) + self.recv[f, s, way, 0].astype(F32)
                ).astype(BF16)
                copies[2].start()

        def finalize(self, store):
            s = self.s
            for f in range(2):
                p = position(f, self.level)
                both = [entry[3] for entry in self.plan if entry[0] == f]
                for h in range(2):
                    both[1 - h][1].wait_recv()
                    both[h][2].wait_recv()
                    total = (
                        self.chunk(f, s, p, h)[...].astype(F32)
                        + self.recv[f, s, h, 2].astype(F32)
                        + self.recv[f, s, 1 - h, 1].astype(F32)
                    )
                    store(f, s, h, total)

        def drain(self):
            for f, way, near, copies in self.plan:
                for copy in copies:
                    copy.wait_send()

    def store_a(f, s, h, total):
        kept[f, s, :, h] = total.astype(BF16)

    def store_b(f, s, h, total):
        last[f, s, h] = total
        last_half[f, s, h] = total.astype(BF16)

    first = [Ring(0, s, chunk_a, ra, acc_a, sa, qa) for s in range(2)]
    second = [Ring(1, s, chunk_b, rb, acc_b, sb, qb) for s in range(2)]
    swaps = [
        [remote(last_half.at[f, s, 1 - me.zh], rc.at[f, s], sc.at[f, s], qc.at[f, s], me.across()) for f in range(2)]
        for s in range(2)
    ]
    first[0].start(0)
    first[0].start(1)
    first[1].start(0)
    pump(1)
    while_first()
    pump(1)
    first[0].accumulate()
    first[1].start(1)
    pump(1)
    first[1].accumulate()
    pump(1)
    first[0].finalize(store_a)
    second[0].start(0)
    second[0].start(1)
    pump(1)
    while_second()
    second[0].accumulate()
    pump(1)
    first[1].finalize(store_a)
    second[1].start(0)
    second[1].start(1)
    second[0].finalize(store_b)
    for swap in swaps[0]:
        swap.start()
    second[1].accumulate()
    second[1].finalize(store_b)
    for swap in swaps[1]:
        swap.start()
    sums = {}
    for s in range(2):
        for f in range(2):
            swaps[s][f].wait_recv()
            sums[f, s] = last[f, s, me.zh] + rc[f, s].astype(F32)
    for ring in first + second:
        ring.drain()
    for swap in swaps[0] + swaps[1]:
        swap.wait_send()
    return [(pl.ds(f * HALF + s * PART, PART), sums[f, s]) for f in range(2) for s in range(2)]


def reduce_scratch():
    dma = pltpu.SemaphoreType.DMA
    bufs = [
        pltpu.VMEM((2, 2, 2, 3, 4, 16, PART), BF16),
        pltpu.VMEM((2, 2, 2, 4, 16, PART), BF16),
        pltpu.VMEM((2, 2, 2, 3, 16, PART), BF16),
        pltpu.VMEM((2, 2, 2, 16, PART), BF16),
        pltpu.VMEM((2, 2, 4, 2, 16, PART), BF16),
        pltpu.VMEM((2, 2, 2, 16, PART), F32),
        pltpu.VMEM((2, 2, 2, 16, PART), BF16),
        pltpu.VMEM((2, 2, 16, PART), BF16),
    ]
    sems = [dma((2, 2, 2, 3))] * 4 + [dma((2, 2))] * 2
    return bufs, sems


class Relay:
    def __init__(self, me, source, stage, parts, sems):
        self.me, self.source, self.stage, self.parts = me, source, stage, parts
        self.s, self.own, self.r, self.zs, self.zr, self.cs, self.cr, self.ps, self.pr = sems

    def hop(self, turn):
        line = turn // 2
        return turn % 2, line + (line // 2) * (5 - 2 * line)

    def holder(self, step):
        me = self.me
        apart, dx = self.hop(step // 4)
        other = ((me.x + dx) % 4) * 8 + ((me.zh + apart) % 2) * 4 + (me.y + step) % 4
        return other, apart, ((me.zl + apart) % 2) * 2 + me.core

    def slot(self, turn):
        apart, dx = self.hop(turn)
        return apart * 4 + (self.me.x + 4 - dx) % 4

    def group(self, slot, flip_z, flip_c):
        me = self.me
        apart = slot // 4
        zl = (me.zl + apart + flip_z) % 2
        core = (me.core + flip_c) % 2
        return (zl * 2 + core) * 8 + (slot % 4) * 2 + (me.zh + apart) % 2

    def at(self, group, part=None, rows=None):
        ref = self.stage
        if len(ref.shape) == 4:
            span = slice(None) if part is None else self.parts[part]
            return ref.at[span, group] if rows is None else ref.at[span, group, rows]
        return ref.at[group] if rows is None else ref.at[group, rows]

    def own_piece(self):
        me = self.me
        mine = me.dp * 8 + me.x * 2 + me.zh
        return self.at(mine, rows=pl.ds(pl.multiple_of(me.y * 32, 32), 32))

    def send(self, batch):
        me = self.me

        def body(step, carry):
            other, apart, group = self.holder(step)
            remote(
                self.source.at[other],
                self.own_piece(),
                self.s.at[batch],
                self.r.at[apart * 4 + me.x],
                (group, other),
            ).start()
            return carry

        if batch == 0:
            pltpu.make_async_copy(self.source.at[me.t], self.own_piece(), self.own).start()
        lax.fori_loop(max(1, 8 * batch), 8 * batch + 8, body, 0)

    def sent(self, batch):
        pieces = self.source.at[pl.ds(0, 7 if batch == 0 else 8)]
        remote(pieces, pieces, self.s.at[batch], self.s.at[batch], (self.me.core_pair, self.me.t)).wait_send()

    def settle(self):
        pltpu.make_async_copy(self.source.at[self.me.t], self.own_piece(), self.own).wait()

    def wait_slot(self, slot):
        me = self.me
        group = self.group(slot, 0, 0)

        def got(count):
            ref = self.at(group, rows=pl.ds(0, count))
            remote(ref, ref, self.s.at[0], self.r.at[slot], (me.core_pair, me.t)).wait_recv()

        @pl.when(slot != me.x)
        def _():
            got(128)

        @pl.when(slot == me.x)
        def _():
            got(96)

    def to_z(self, slot, part=0):
        ref = self.at(self.group(slot, 0, 0), part)
        return remote(ref, ref, self.zs.at[part, slot], self.zr.at[part, slot], (self.me.z_pair, self.me.t))

    def to_core(self, slot):
        ref = self.at(self.group(slot, 0, 0))
        return remote(ref, ref, self.cs.at[slot], self.cr.at[slot], (self.me.core_pair, self.me.t))

    def pass_on(self, slot, part=0):
        ref = self.at(self.group(slot, 1, 0), part)
        return remote(ref, ref, self.ps.at[part, slot], self.pr.at[part, slot], (self.me.core_pair, self.me.t))

    def got(self, ref, sem):
        remote(ref, ref, self.s.at[0], sem, (self.me.core_pair, self.me.t)).wait_recv()

    def each(self, first, last, act):
        def body(turn, carry):
            act(self.slot(turn))
            return carry

        lax.fori_loop(first, last, body, 0)

    def forward(self, first, last):
        def act(slot):
            self.wait_slot(slot)
            self.to_z(slot).start()
            self.to_core(slot).start()

        self.each(first, last, act)

    def relay_on(self, first, last, part=0):
        def act(slot):
            self.got(self.at(self.group(slot, 1, 0), part), self.zr.at[part, slot])
            self.pass_on(slot, part).start()

        self.each(first, last, act)

    def cores(self):
        self.each(0, 8, lambda slot: self.got(self.at(self.group(slot, 0, 1)), self.cr.at[slot]))

    def complete(self, part=0):
        self.each(
            0, 8, lambda slot: self.got(self.at(self.group(slot, 1, 1), part), self.pr.at[part, slot])
        )

    def drain(self):
        def act(slot):
            self.to_core(slot).wait_send()
            for part in range(len(self.parts)):
                self.to_z(slot, part).wait_send()
                self.pass_on(slot, part).wait_send()

        self.each(0, 8, act)


def norm_rows(values, gain):
    center = values - jnp.mean(values, axis=-1, keepdims=True)
    spread = jnp.mean(center * center, axis=-1, keepdims=True)
    return (center * lax.rsqrt(spread + EPSILON) * gain).astype(BF16)


def gather_rows(me, field, view, axes, s_sem, r_sem, pump):
    plan = []
    for f in range(2):
        axis = axes[f]
        p = me.x if axis == "x" else me.y
        for way in range(2):
            delta = 1 - 2 * way
            device = me.near(axis, delta)
            unit = view(f, p, None)
            came = view(f, (p + 4 - delta) % 4, way)
            plan.append(
                (
                    remote(unit, unit, s_sem.at[f, way, 0], r_sem.at[f, way, 0], device),
                    remote(came, came, s_sem.at[f, way, 1], r_sem.at[f, way, 1], device),
                )
            )
    for whole, half in plan:
        whole.start()
    pump(2)
    for whole, half in plan:
        whole.wait_recv()
        half.start()
    pump(1)
    for whole, half in plan:
        half.wait_recv()
    for whole, half in plan:
        whole.wait_send()
        half.wait_send()


def attend(queries, keys, values, seg, slope, context):
    scale = 1.0 / math.sqrt(HD)
    for block in range(4):
        rows = pl.ds(block * 128, 128)
        reach = (block + 1) * 128
        cols = pl.ds(0, reach)
        scores = (
            lax.dot_general(
                queries[rows, :], keys[cols, :], (((1,), (1,)), ((), ())), preferred_element_type=F32
            )
            * scale
        )
        n = lax.broadcasted_iota(jnp.int32, (128, reach), 0) + block * 128
        p = lax.broadcasted_iota(jnp.int32, (128, reach), 1)
        scores = scores - slope * (n - p).astype(F32)
        own = jnp.broadcast_to(seg[:, rows], (128, 128)).T[:, 0:1]
        allowed = (own == seg[:, cols]) & (p <= n)
        scores = jnp.where(allowed, scores, -jnp.inf)
        highest = jnp.max(scores, axis=-1, keepdims=True)
        raised = jnp.exp(scores - highest)
        weights = (raised / jnp.sum(raised, axis=-1, keepdims=True)).astype(BF16)
        context[rows, :] = jnp.dot(weights, values[cols, :], preferred_element_type=F32).astype(BF16)


def layer_kernel(*refs):
    (hidden, seg, slope, gain_one, gain_two, q_in, o_in, u_in, w_in) = refs[:9]
    (result, k_v, v_v, qo, turned, up, normed) = refs[9:16]
    rest = refs[16:]
    (q_f, o_f, u_f, w_f, h_v, sq, su, sw, down, field, share, acc, q_v, ctx, act, middle) = rest[:16]
    in_sem = rest[16]
    relay_sems = [rest[17 + 9 * k : 26 + 9 * k] for k in range(3)]
    rest = rest[44:]
    bufs_one, sems_one, bufs_two, sems_two = rest[:8], rest[8:14], rest[14:22], rest[22:28]
    a_s, a_r, b_s, b_r, x_s, x_r = rest[28:]
    me = Place()

    loads = [
        pltpu.make_async_copy(src, dst, in_sem.at[k])
        for k, (src, dst) in enumerate(
            ((q_in, q_f), (o_in, o_f), (u_in, u_f), (w_in, w_f), (hidden, h_v))
        )
    ]
    loads[0].start()
    loads[1].start()
    r_q = Relay(me, sq, qo, (pl.ds(0, 3), pl.ds(3, 1)), relay_sems[0])
    r_u = Relay(me, su, up, (None,), relay_sems[1])
    r_d = Relay(me, sw, down, (None,), relay_sems[2])

    barrier = pltpu.get_barrier_semaphore()

    def hello(step, carry):
        other, _, group = r_q.holder(step)
        greet(barrier, (group, other))
        return carry

    lax.fori_loop(1, 32, hello, 0)
    greet(barrier, (me.z_pair, me.t))
    greet(barrier, (me.core_pair, me.t))
    greet(barrier, me.across())
    loads[0].wait()
    loads[1].wait()
    for load in loads[2:]:
        load.start()

    @pl.loop(0, 32)
    def _(part):
        cols = pl.ds(pl.multiple_of(part * 128, 128), 128)
        sq[part, 0:3] = q_f[:, :, cols].astype(BF16)
        sq[part, 3] = o_f[:, cols].astype(BF16)

    pl.semaphore_wait(barrier, 34)
    r_q.send(0)

    def cast(source, target):
        @pl.loop(0, 32)
        def _(part):
            cols = pl.ds(pl.multiple_of(part * 512, 512), 512)
            target[part] = source[:, cols].astype(BF16)

    r_q.sent(0)
    r_q.send(1)
    r_q.send(2)
    r_q.settle()
    r_q.forward(0, 2)
    loads[2].wait()
    cast(u_f, su)
    r_q.sent(1)
    r_q.sent(2)
    r_q.send(3)
    r_q.forward(2, 6)
    loads[3].wait()
    cast(w_f, sw)
    r_q.sent(3)
    for batch in range(4):
        r_u.send(batch)
    r_q.forward(6, 8)
    r_q.each(0, 8, lambda slot: r_q.to_z(slot, 1).start())
    loads[4].wait()

    def passing(turn, carry):
        @pl.loop(0, 2)
        def _(part):
            rows = pl.ds(pl.multiple_of(turn * 64 + part * 32, 32), 32)
            normed[rows, :] = norm_rows(h_v[rows, :].astype(F32), gain_one[...])

        r_q.relay_on(turn, turn + 1)
        return carry

    lax.fori_loop(0, 8, passing, 0)
    turns = [(relay, turn) for relay in (r_u, r_d) for turn in range(8)]
    done = [0]

    def pump(count):
        for _ in range(count):
            n = done[0]
            done[0] = n + 1
            if n < 16:
                relay, turn = turns[n]
                slot = relay.slot(turn)
                relay.wait_slot(slot)
                relay.to_z(slot).start()
                relay.to_core(slot).start()
            if n >= 4:
                relay, turn = turns[n - 4]
                relay.relay_on(turn, turn + 1)

    r_u.settle()
    pump(2)
    for batch in range(4):
        r_u.sent(batch)
    for batch in range(4):
        r_d.send(batch)
    r_q.cores()
    r_q.complete()

    acc_q = acc.at[:, pl.ds(0, 384)]
    for part in range(8):
        cols = pl.ds(part * 512, 512)
        block = jnp.concatenate(
            [qo[k, part * 4 : part * 4 + 4].reshape(512, 128) for k in range(3)], axis=1
        )
        product = jnp.dot(normed[:, cols], block, preferred_element_type=F32)
        if part == 0:
            acc_q[...] = product
        else:
            acc_q[...] += product
    pump(1)
    q_v[...] = acc[:, 0:128].astype(BF16)
    k_v[...] = acc[:, 128:256].astype(BF16)
    v_v[...] = acc[:, 256:384].astype(BF16)
    attend(q_v, k_v, v_v, seg, slope[0:1, 0:1], ctx)
    pump(1)
    r_q.relay_on(0, 8, 1)
    r_q.complete(1)
    r_d.settle()

    @pl.loop(0, 8)
    def _(part):
        block = qo[3, pl.ds(part * 4, 4)].reshape(512, 128)
        product = lax.dot_general(
            ctx[...], block, (((1,), (1,)), ((), ())), preferred_element_type=F32
        ).astype(BF16)
        cols = pl.ds(pl.multiple_of(part * 512, 512), 512)
        share[:, :, :, :, cols] = product.reshape(4, 2, 4, 16, 512)

    pump(1)

    def turn_out(first, last):
        @pl.loop(first, last)
        def _(part):
            cols = pl.ds(pl.multiple_of(part * 128, 128), 128)
            turned[:, cols] = qo[3, part].T

    def turn_down(first, last):
        @pl.loop(first, last)
        def _(part):
            cols = pl.ds(pl.multiple_of(part * 128, 128), 128)
            normed[:, cols] = down[part].T

    own_rows = pl.ds(pl.multiple_of(me.t * 16, 16), 16)
    for cols, total in reduce_rows(
        me, share, bufs_one, sems_one, lambda: turn_out(0, 32), lambda: None, pump
    ):
        middle[:, cols] = (h_v[own_rows, cols].astype(F32) + total).astype(BF16)
    field[me.x, me.zh, me.y] = norm_rows(middle[...].astype(F32), gain_two[...])

    spot = field.at[me.x, me.zh, me.y]
    swap = remote(spot, spot, x_s, x_r, me.across())
    swap.start()
    swap.wait_recv()
    swap.wait_send()

    def view_b(f, q, h):
        cols = pl.ds(f * HALF, HALF)
        lane = slice(None) if h is None else h
        if f == 0:
            return field.at[me.x, lane, q, :, cols]
        return field.at[q, lane, me.y, :, cols]

    def view_a(f, q, h):
        cols = pl.ds(f * HALF, HALF)
        lane = slice(None) if h is None else h
        if f == 0:
            return field.at[q, lane, :, :, cols]
        return field.at[:, lane, q, :, cols]

    gather_rows(me, field, view_b, ("y", "x"), b_s, b_r, pump)
    gather_rows(me, field, view_a, ("x", "y"), a_s, a_r, pump)
    pump(20 - done[0])
    r_u.cores()
    r_u.complete()

    for part in range(8):
        rows = field[:, :, :, :, part * 512 : part * 512 + 512].reshape(512, 512)
        block = up[part * 4 : part * 4 + 4].reshape(512, 512)
        product = jnp.dot(rows, block, preferred_element_type=F32)
        if part == 0:
            acc[...] = product
        else:
            acc[...] += product

    @pl.loop(0, 8)
    def _(part):
        rows = pl.ds(pl.multiple_of(part * 64, 64), 64)
        values = acc[rows, :]
        act[rows, :] = (0.5 * values * (1.0 + lax.erf(values * math.sqrt(0.5)))).astype(BF16)

    r_d.cores()
    r_d.complete()

    @pl.loop(0, 8)
    def _(part):
        block = down[pl.ds(part * 4, 4)].reshape(512, 512)
        product = lax.dot_general(
            act[...], block, (((1,), (1,)), ((), ())), preferred_element_type=F32
        ).astype(BF16)
        cols = pl.ds(pl.multiple_of(part * 512, 512), 512)
        share[:, :, :, :, cols] = product.reshape(4, 2, 4, 16, 512)


    for cols, total in reduce_rows(
        me, share, bufs_two, sems_two, lambda: turn_down(0, 16), lambda: turn_down(16, 32)
    ):
        result[:, cols] = (middle[:, cols].astype(F32) + total).astype(BF16)
    for batch in range(4):
        r_d.sent(batch)
    for relay in (r_q, r_u, r_d):
        relay.drain()


def layer(hidden, seg, slope, gain_one, gain_two, qkv, out, up, down):
    any_spec = pl.BlockSpec(memory_space=pl.ANY)
    vmem = pl.BlockSpec(memory_space=pltpu.VMEM)
    dma = pltpu.SemaphoreType.DMA
    bufs_one, sems_one = reduce_scratch()
    bufs_two, sems_two = reduce_scratch()
    def relay_sems(parts):
        one, many = dma((8,)), dma((parts, 8))
        return [dma((4,)), dma(()), one, many, many, one, one, many, many]

    return pl.pallas_call(
        layer_kernel,
        out_shape=(
            pltpu.VMEM((16, D), BF16),
            pltpu.VMEM((512, HD), BF16),
            pltpu.VMEM((512, HD), BF16),
            pltpu.VMEM((4, 32, 128, HD), BF16),
            pltpu.VMEM((HD, D), BF16),
            pltpu.VMEM((32, 128, 512), BF16),
            pltpu.VMEM((512, D), BF16),
        ),
        in_specs=[any_spec, vmem, vmem, vmem, vmem] + [any_spec] * 4,
        out_specs=[vmem] * 7,
        scratch_shapes=[
            pltpu.VMEM((3, 32, 4096), F32),
            pltpu.VMEM((32, 4096), F32),
            pltpu.VMEM((32, 16384), F32),
            pltpu.VMEM((32, 16384), F32),
            pltpu.VMEM((512, D), BF16),
            pltpu.VMEM((32, 4, 32, 128), BF16),
            pltpu.VMEM((32, 32, 512), BF16),
            pltpu.VMEM((32, 32, 512), BF16),
            pltpu.VMEM((32, 128, 512), BF16),
            pltpu.VMEM((4, 2, 4, 16, D), BF16),
            pltpu.VMEM((4, 2, 4, 16, D), BF16),
            pltpu.VMEM((512, 512), F32),
            pltpu.VMEM((512, HD), BF16),
            pltpu.VMEM((512, HD), BF16),
            pltpu.VMEM((512, 512), BF16),
            pltpu.VMEM((16, D), BF16),
            dma((5,)),
        ]
        + relay_sems(2)
        + relay_sems(1)
        + relay_sems(1)
        + bufs_one
        + sems_one
        + bufs_two
        + sems_two
        + [dma((2, 2, 2))] * 4
        + [dma(()), dma(())],
        compiler_params=pltpu.CompilerParams(
            collective_id=0, has_side_effects=True, vmem_limit_bytes=46 << 20
        ),
        name="layer",
    )(hidden, seg.reshape(1, 512), slope, gain_one, gain_two, qkv, out, up, down)


def store_kernel(*refs):
    sem = refs[14]
    copies = [
        pltpu.make_async_copy(refs[k].at[pl.ds(0, refs[7 + k].shape[0])], refs[7 + k], sem.at[k])
        for k in range(7)
    ]
    for copy in copies:
        copy.start()
    for copy in copies:
        copy.wait()


def store(values):
    any_spec = pl.BlockSpec(memory_space=pl.ANY)
    vmem = pl.BlockSpec(memory_space=pltpu.VMEM)
    return pl.pallas_call(
        store_kernel,
        out_shape=[
            jax.ShapeDtypeStruct((3,) + value.shape[1:] if k == 3 else value.shape, value.dtype)
            for k, value in enumerate(values)
        ],
        in_specs=[any_spec] * 7,
        out_specs=[any_spec] * 7,
        scratch_shapes=[pltpu.SemaphoreType.DMA((7,))],
        compiler_params=pltpu.CompilerParams(vmem_limit_bytes=1 << 20),
        name="store",
    )(*values)


def shards(
    hidden, segment_ids, first_gain, second_gain, qkv_master, out_master, up_master, down_master
):
    slope = jnp.exp2(-8.0 * (lax.axis_index("tensor").astype(F32) + 1.0) / (D // HD))
    made = layer(
        hidden,
        segment_ids,
        jnp.full((1, 128), slope, F32),
        first_gain.reshape(1, D),
        second_gain.reshape(1, D),
        qkv_master.transpose(1, 0, 2),
        out_master.T,
        up_master,
        down_master.T,
    )
    new_hidden, keys, values, qkv, out_block, up, down_block = store(made)
    return (
        new_hidden,
        keys,
        values,
        qkv.reshape(3, D, HD).transpose(1, 0, 2),
        out_block,
        up.reshape(D, 512),
        down_block,
    )


def solution(mesh):
    in_specs = (
        P("dp", None),
        P("dp"),
        P(),
        P(),
        P(("dp", "tensor"), None, None),
        P(None, ("dp", "tensor")),
        P(("dp", "tensor"), None),
        P(None, ("dp", "tensor")),
    )
    out_specs = (
        P(("dp", "tensor"), None),
        P("dp", "tensor"),
        P("dp", "tensor"),
        P(None, None, "tensor"),
        P("tensor", None),
        P(None, "tensor"),
        P("tensor", None),
    )
    return jax.shard_map(shards, mesh=mesh, in_specs=in_specs, out_specs=out_specs, check_vma=False)
```

```python
import math

import jax
import jax.numpy as jnp
from jax import lax
from jax.experimental import pallas as pl
from jax.experimental.pallas import tpu as pltpu
from jax.sharding import PartitionSpec as P

D = 4096
HD = 128
EPSILON = 1e-05
MESH = pl.DeviceIdType.MESH
BF16 = jnp.bfloat16
F32 = jnp.float32


class Place:
    def __init__(self):
        self.dp = lax.axis_index("dp")
        self.t = lax.axis_index("tensor")
        self.zl = self.dp // 2
        self.core = self.dp % 2
        self.x = self.t // 8
        self.zh = (self.t // 4) % 2
        self.y = self.t % 4
        self.z_pair = (1 - self.zl) * 2 + self.core
        self.core_pair = self.zl * 2 + (1 - self.core)

    def near(self, axis, delta):
        if axis == "x":
            return (self.dp, ((self.x + delta) % 4) * 8 + self.zh * 4 + self.y)
        return (self.dp, self.x * 8 + self.zh * 4 + (self.y + delta) % 4)

    def across(self):
        return (self.dp, self.x * 8 + (1 - self.zh) * 4 + self.y)


def remote(src, dst, send_sem, recv_sem, device):
    return pltpu.make_async_remote_copy(
        src_ref=src,
        dst_ref=dst,
        send_sem=send_sem,
        recv_sem=recv_sem,
        device_id=device,
        device_id_type=MESH,
    )


def greet(barrier, device):
    pl.semaphore_signal(barrier, inc=1, device_id=device, device_id_type=MESH)


HALF = 2048
PART = 1024


def reduce_rows(me, share, bufs, sems, fill, while_first, while_second, pump=lambda count: None):
    ra, acc_a, rb, acc_b, kept, last, last_half, rc = bufs
    sa, qa, sb, qb, sc, qc = sems
    axes = (("x", "y"), ("y", "x"))

    def chunk_a(f, s, q, h):
        cols = pl.ds(f * HALF + s * PART, PART)
        if f == 0:
            return share.at[q, h, :, :, cols]
        return share.at[:, h, q, :, cols]

    def chunk_b(f, s, q, h):
        return kept.at[f, s, q, h]

    def position(f, level):
        return me.x if axes[f][level] == "x" else me.y

    class Ring:
        def __init__(self, level, s, chunk, recv, acc, s_sem, r_sem):
            self.level, self.s, self.chunk, self.recv, self.acc = level, s, chunk, recv, acc
            self.plan = []
            for f in range(2):
                p = position(f, level)
                far = (p + 2) % 4
                for way in range(2):
                    delta = 1 - 2 * way
                    near = (p + delta) % 4
                    device = me.near(axes[f][level], delta)
                    copies = [
                        remote(src, recv.at[f, s, way, k], s_sem.at[f, s, way, k], r_sem.at[f, s, way, k], device)
                        for k, src in enumerate(
                            (chunk(f, s, far, way), chunk(f, s, near, 1 - way), acc.at[f, s, way])
                        )
                    ]
                    self.plan.append((f, way, near, copies))

        def start(self, k):
            for f, way, near, copies in self.plan:
                copies[k].start()

        def accumulate(self):
            s = self.s
            for f, way, near, copies in self.plan:
                copies[0].wait_recv()
                self.acc[f, s, way] = (
                    self.chunk(f, s, near, way)[...].astype(F32) + self.recv[f, s, way, 0].astype(F32)
                ).astype(BF16)
                copies[2].start()

        def finalize(self, store):
            s = self.s
            for f in range(2):
                p = position(f, self.level)
                both = [entry[3] for entry in self.plan if entry[0] == f]
                for h in range(2):
                    both[1 - h][1].wait_recv()
                    both[h][2].wait_recv()
                    total = (
                        self.chunk(f, s, p, h)[...].astype(F32)
                        + self.recv[f, s, h, 2].astype(F32)
                        + self.recv[f, s, 1 - h, 1].astype(F32)
                    )
                    store(f, s, h, total)

        def drain(self):
            for f, way, near, copies in self.plan:
                for copy in copies:
                    copy.wait_send()

    def store_a(f, s, h, total):
        kept[f, s, :, h] = total.astype(BF16)

    def store_b(f, s, h, total):
        last[f, s, h] = total
        last_half[f, s, h] = total.astype(BF16)

    first = [Ring(0, s, chunk_a, ra, acc_a, sa, qa) for s in range(2)]
    second = [Ring(1, s, chunk_b, rb, acc_b, sb, qb) for s in range(2)]
    swaps = [
        [remote(last_half.at[f, s, 1 - me.zh], rc.at[f, s], sc.at[f, s], qc.at[f, s], me.across()) for f in range(2)]
        for s in range(2)
    ]
    fill(0)
    first[0].start(0)
    first[0].start(1)
    pump(1)
    fill(1)
    first[1].start(0)
    while_first()
    pump(1)
    first[0].accumulate()
    first[1].start(1)
    pump(1)
    first[1].accumulate()
    pump(1)
    first[0].finalize(store_a)
    second[0].start(0)
    second[0].start(1)
    pump(1)
    while_second()
    second[0].accumulate()
    pump(1)
    first[1].finalize(store_a)
    second[1].start(0)
    second[1].start(1)
    second[0].finalize(store_b)
    for swap in swaps[0]:
        swap.start()
    second[1].accumulate()
    second[1].finalize(store_b)
    for swap in swaps[1]:
        swap.start()
    sums = {}
    for s in range(2):
        for f in range(2):
            swaps[s][f].wait_recv()
            sums[f, s] = last[f, s, me.zh] + rc[f, s].astype(F32)
    for ring in first + second:
        ring.drain()
    for swap in swaps[0] + swaps[1]:
        swap.wait_send()
    return [(pl.ds(f * HALF + s * PART, PART), sums[f, s]) for f in range(2) for s in range(2)]


def reduce_scratch():
    dma = pltpu.SemaphoreType.DMA
    bufs = [
        pltpu.VMEM((2, 2, 2, 3, 4, 16, PART), BF16),
        pltpu.VMEM((2, 2, 2, 4, 16, PART), BF16),
        pltpu.VMEM((2, 2, 2, 3, 16, PART), BF16),
        pltpu.VMEM((2, 2, 2, 16, PART), BF16),
        pltpu.VMEM((2, 2, 4, 2, 16, PART), BF16),
        pltpu.VMEM((2, 2, 2, 16, PART), F32),
        pltpu.VMEM((2, 2, 2, 16, PART), BF16),
        pltpu.VMEM((2, 2, 16, PART), BF16),
    ]
    sems = [dma((2, 2, 2, 3))] * 4 + [dma((2, 2))] * 2
    return bufs, sems


class Relay:
    def __init__(self, me, source, stage, parts, sems):
        self.me, self.source, self.stage, self.parts = me, source, stage, parts
        self.s, self.own, self.r, self.zs, self.zr, self.cs, self.cr, self.ps, self.pr = sems

    def hop(self, turn):
        line = turn // 2
        return turn % 2, line + (line // 2) * (5 - 2 * line)

    def holder(self, step):
        me = self.me
        apart, dx = self.hop(step // 4)
        other = ((me.x + dx) % 4) * 8 + ((me.zh + apart) % 2) * 4 + (me.y + step) % 4
        return other, apart, ((me.zl + apart) % 2) * 2 + me.core

    def slot(self, turn):
        apart, dx = self.hop(turn)
        return apart * 4 + (self.me.x + 4 - dx) % 4

    def group(self, slot, flip_z, flip_c):
        me = self.me
        apart = slot // 4
        zl = (me.zl + apart + flip_z) % 2
        core = (me.core + flip_c) % 2
        return (zl * 2 + core) * 8 + (slot % 4) * 2 + (me.zh + apart) % 2

    def at(self, group, part=None, rows=None):
        ref = self.stage
        if len(ref.shape) == 4:
            span = slice(None) if part is None else self.parts[part]
            return ref.at[span, group] if rows is None else ref.at[span, group, rows]
        return ref.at[group] if rows is None else ref.at[group, rows]

    def own_piece(self):
        me = self.me
        mine = me.dp * 8 + me.x * 2 + me.zh
        return self.at(mine, rows=pl.ds(pl.multiple_of(me.y * 32, 32), 32))

    def send(self, batch):
        me = self.me

        def body(step, carry):
            other, apart, group = self.holder(step)
            remote(
                self.source.at[other],
                self.own_piece(),
                self.s.at[batch],
                self.r.at[apart * 4 + me.x],
                (group, other),
            ).start()
            return carry

        if batch == 0:
            pltpu.make_async_copy(self.source.at[me.t], self.own_piece(), self.own).start()
        lax.fori_loop(max(1, 8 * batch), 8 * batch + 8, body, 0)

    def sent(self, batch):
        pieces = self.source.at[pl.ds(0, 7 if batch == 0 else 8)]
        remote(pieces, pieces, self.s.at[batch], self.s.at[batch], (self.me.core_pair, self.me.t)).wait_send()

    def settle(self):
        pltpu.make_async_copy(self.source.at[self.me.t], self.own_piece(), self.own).wait()

    def wait_slot(self, slot):
        me = self.me
        group = self.group(slot, 0, 0)

        def got(count):
            ref = self.at(group, rows=pl.ds(0, count))
            remote(ref, ref, self.s.at[0], self.r.at[slot], (me.core_pair, me.t)).wait_recv()

        @pl.when(slot != me.x)
        def _():
            got(128)

        @pl.when(slot == me.x)
        def _():
            got(96)

    def to_z(self, slot, part=0):
        ref = self.at(self.group(slot, 0, 0), part)
        return remote(ref, ref, self.zs.at[part, slot], self.zr.at[part, slot], (self.me.z_pair, self.me.t))

    def to_core(self, slot):
        ref = self.at(self.group(slot, 0, 0))
        return remote(ref, ref, self.cs.at[slot], self.cr.at[slot], (self.me.core_pair, self.me.t))

    def pass_on(self, slot, part=0):
        ref = self.at(self.group(slot, 1, 0), part)
        return remote(ref, ref, self.ps.at[part, slot], self.pr.at[part, slot], (self.me.core_pair, self.me.t))

    def got(self, ref, sem):
        remote(ref, ref, self.s.at[0], sem, (self.me.core_pair, self.me.t)).wait_recv()

    def each(self, first, last, act):
        def body(turn, carry):
            act(self.slot(turn))
            return carry

        lax.fori_loop(first, last, body, 0)

    def forward(self, first, last):
        def act(slot):
            self.wait_slot(slot)
            self.to_z(slot).start()
            self.to_core(slot).start()

        self.each(first, last, act)

    def relay_on(self, first, last, part=0):
        def act(slot):
            self.got(self.at(self.group(slot, 1, 0), part), self.zr.at[part, slot])
            self.pass_on(slot, part).start()

        self.each(first, last, act)

    def cores(self):
        self.each(0, 8, lambda slot: self.got(self.at(self.group(slot, 0, 1)), self.cr.at[slot]))

    def complete(self, part=0):
        self.each(
            0, 8, lambda slot: self.got(self.at(self.group(slot, 1, 1), part), self.pr.at[part, slot])
        )

    def drain(self):
        def act(slot):
            self.to_core(slot).wait_send()
            for part in range(len(self.parts)):
                self.to_z(slot, part).wait_send()
                self.pass_on(slot, part).wait_send()

        self.each(0, 8, act)


def norm_rows(values, gain):
    center = values - jnp.mean(values, axis=-1, keepdims=True)
    spread = jnp.mean(center * center, axis=-1, keepdims=True)
    return (center * lax.rsqrt(spread + EPSILON) * gain).astype(BF16)


def gather_rows(me, field, swap, sems, pump):
    a_s, a_r, b_s, b_r = sems

    def view_b(f, part, q, half):
        z = me.zh if part == 0 else 1 - me.zh
        cols = pl.ds(f * HALF, HALF) if half is None else pl.ds(f * HALF + half * PART, PART)
        if f == 0:
            return field.at[me.x, z, q, :, cols]
        return field.at[q, z, me.y, :, cols]

    def view_a(f, part, q, half):
        z = me.zh if part == 0 else 1 - me.zh
        cols = pl.ds(f * HALF, HALF)
        some = slice(None) if half is None else pl.ds(2 * half, 2)
        if f == 0:
            return field.at[q, z, some, :, cols]
        return field.at[some, z, q, :, cols]

    def ring(part, view, axes, s_sem, r_sem):
        plan = []
        for f in range(2):
            axis = axes[f]
            p = me.x if axis == "x" else me.y
            for way in range(2):
                delta = 1 - 2 * way
                device = me.near(axis, delta)
                unit = view(f, part, p, None)
                came = view(f, part, (p + 4 - delta) % 4, way)
                at = (part, f, way)
                plan.append(
                    (
                        remote(unit, unit, s_sem.at[at + (0,)], r_sem.at[at + (0,)], device),
                        remote(came, came, s_sem.at[at + (1,)], r_sem.at[at + (1,)], device),
                    )
                )
        return plan

    def begin(plan):
        for whole, half in plan:
            whole.start()

    def turn(plan):
        for whole, half in plan:
            whole.wait_recv()
            half.start()

    def end(plan):
        for whole, half in plan:
            half.wait_recv()

    near = [ring(part, view_b, ("y", "x"), b_s, b_r) for part in range(2)]
    wide = [ring(part, view_a, ("x", "y"), a_s, a_r) for part in range(2)]
    swap.start()
    begin(near[0])
    swap.wait_recv()
    begin(near[1])
    pump(2)
    turn(near[0])
    turn(near[1])
    end(near[0])
    begin(wide[0])
    end(near[1])
    begin(wide[1])
    pump(2)
    turn(wide[0])
    pump(1)
    turn(wide[1])
    pump(1)
    end(wide[0])
    end(wide[1])
    for plan in near + wide:
        for whole, half in plan:
            whole.wait_send()
            half.wait_send()
    swap.wait_send()


def attend(queries, keys, values, seg, slope, context):
    scale = 1.0 / math.sqrt(HD)
    for block in range(4):
        rows = pl.ds(block * 128, 128)
        reach = (block + 1) * 128
        cols = pl.ds(0, reach)
        scores = (
            lax.dot_general(
                queries[rows, :], keys[cols, :], (((1,), (1,)), ((), ())), preferred_element_type=F32
            )
            * scale
        )
        n = lax.broadcasted_iota(jnp.int32, (128, reach), 0) + block * 128
        p = lax.broadcasted_iota(jnp.int32, (128, reach), 1)
        scores = scores - slope * (n - p).astype(F32)
        own = jnp.broadcast_to(seg[:, rows], (128, 128)).T[:, 0:1]
        allowed = (own == seg[:, cols]) & (p <= n)
        scores = jnp.where(allowed, scores, -jnp.inf)
        highest = jnp.max(scores, axis=-1, keepdims=True)
        raised = jnp.exp(scores - highest)
        weights = (raised / jnp.sum(raised, axis=-1, keepdims=True)).astype(BF16)
        context[rows, :] = jnp.dot(weights, values[cols, :], preferred_element_type=F32).astype(BF16)


def layer_kernel(*refs):
    (hidden, seg, gain_one, gain_two, q_in, o_in, u_in, w_in) = refs[:8]
    (result, k_v, v_v, qo, turned, up, normed) = refs[8:15]
    rest = refs[15:]
    (q_f, o_f, u_f, w_f, h_v, sq, su, sw, down, field, share, acc, q_v, ctx, act, middle) = rest[:16]
    in_sem = rest[16]
    relay_sems = [rest[17 + 9 * k : 26 + 9 * k] for k in range(3)]
    rest = rest[44:]
    bufs_one, sems_one, bufs_two, sems_two = rest[:8], rest[8:14], rest[14:22], rest[22:28]
    a_s, a_r, b_s, b_r, x_s, x_r = rest[28:]
    me = Place()

    loads = [
        pltpu.make_async_copy(src, dst, in_sem.at[k])
        for k, (src, dst) in enumerate(
            ((q_in, q_f), (o_in, o_f), (u_in, u_f), (w_in, w_f), (hidden, h_v))
        )
    ]
    loads[0].start()
    loads[1].start()
    r_q = Relay(me, sq, qo, (pl.ds(0, 3), pl.ds(3, 1)), relay_sems[0])
    r_u = Relay(me, su, up, (None,), relay_sems[1])
    r_d = Relay(me, sw, down, (None,), relay_sems[2])

    barrier = pltpu.get_barrier_semaphore()

    def hello(step, carry):
        other, _, group = r_q.holder(step)
        greet(barrier, (group, other))
        return carry

    lax.fori_loop(1, 32, hello, 0)
    greet(barrier, (me.z_pair, me.t))
    greet(barrier, (me.core_pair, me.t))
    greet(barrier, me.across())
    loads[0].wait()
    loads[1].wait()
    for load in loads[2:]:
        load.start()

    @pl.loop(0, 32)
    def _(part):
        cols = pl.ds(pl.multiple_of(part * 128, 128), 128)
        sq[part, 0:3] = q_f[:, :, cols].astype(BF16)
        sq[part, 3] = o_f[:, cols].astype(BF16)

    pl.semaphore_wait(barrier, 34)
    r_q.send(0)

    def cast(source, target):
        @pl.loop(0, 32)
        def _(part):
            cols = pl.ds(pl.multiple_of(part * 512, 512), 512)
            target[part] = source[:, cols].astype(BF16)

    r_q.sent(0)
    r_q.send(1)
    r_q.send(2)
    r_q.settle()
    r_q.forward(0, 2)
    loads[2].wait()
    cast(u_f, su)
    r_q.sent(1)
    r_q.sent(2)
    r_q.send(3)
    r_q.forward(2, 6)
    loads[3].wait()
    cast(w_f, sw)
    r_q.sent(3)
    for batch in range(4):
        r_u.send(batch)
    r_q.forward(6, 8)
    r_q.each(0, 8, lambda slot: r_q.to_z(slot, 1).start())
    loads[4].wait()

    def passing(turn, carry):
        @pl.loop(0, 2)
        def _(part):
            rows = pl.ds(pl.multiple_of(turn * 64 + part * 32, 32), 32)
            normed[rows, :] = norm_rows(h_v[rows, :].astype(F32), gain_one[...])

        r_q.relay_on(turn, turn + 1)
        return carry

    lax.fori_loop(0, 4, passing, 0)
    for batch in range(4):
        passing(4 + batch, 0)
        r_u.sent(batch)
        r_d.send(batch)
    turns = [(relay, turn) for relay in (r_u, r_d) for turn in range(8)]
    done = [0]

    def pump(count):
        for _ in range(count):
            n = done[0]
            done[0] = n + 1
            if n < 16:
                relay, turn = turns[n]
                slot = relay.slot(turn)
                relay.wait_slot(slot)
                relay.to_z(slot).start()
                relay.to_core(slot).start()
            if n >= 4:
                relay, turn = turns[n - 4]
                relay.relay_on(turn, turn + 1)

    r_u.settle()
    pump(2)
    r_q.cores()
    r_q.complete()

    acc_q = acc.at[:, pl.ds(0, 384)]
    for part in range(8):
        cols = pl.ds(part * 512, 512)
        block = jnp.concatenate(
            [qo[k, part * 4 : part * 4 + 4].reshape(512, 128) for k in range(3)], axis=1
        )
        product = jnp.dot(normed[:, cols], block, preferred_element_type=F32)
        if part == 0:
            acc_q[...] = product
        else:
            acc_q[...] += product
    pump(1)
    q_v[...] = acc[:, 0:128].astype(BF16)
    k_v[...] = acc[:, 128:256].astype(BF16)
    v_v[...] = acc[:, 256:384].astype(BF16)
    head = jnp.full((1, 128), me.t + 1, jnp.int32).astype(F32)
    attend(q_v, k_v, v_v, seg, jnp.exp2(-8.0 * head / (D // HD))[:, 0:1], ctx)
    pump(1)
    r_q.relay_on(0, 8, 1)
    r_q.complete(1)
    r_d.settle()

    def columns(i, part):
        return i % 2 + (i // 2) * 4 + 2 * part

    def share_one(part):
        @pl.loop(0, 4)
        def _(i):
            k = columns(i, part)
            block = qo[3, pl.ds(k * 4, 4)].reshape(512, 128)
            product = lax.dot_general(
                ctx[...], block, (((1,), (1,)), ((), ())), preferred_element_type=F32
            ).astype(BF16)
            cols = pl.ds(pl.multiple_of(k * 512, 512), 512)
            share[:, :, :, :, cols] = product.reshape(4, 2, 4, 16, 512)

    def share_two(part):
        @pl.loop(0, 4)
        def _(i):
            k = columns(i, part)
            block = down[pl.ds(k * 4, 4)].reshape(512, 512)
            product = lax.dot_general(
                act[...], block, (((1,), (1,)), ((), ())), preferred_element_type=F32
            ).astype(BF16)
            cols = pl.ds(pl.multiple_of(k * 512, 512), 512)
            share[:, :, :, :, cols] = product.reshape(4, 2, 4, 16, 512)

    pump(1)

    def turn_out(first, last):
        @pl.loop(first, last)
        def _(part):
            cols = pl.ds(pl.multiple_of(part * 128, 128), 128)
            turned[:, cols] = qo[3, part].T

    def turn_down(first, last):
        @pl.loop(first, last)
        def _(part):
            cols = pl.ds(pl.multiple_of(part * 128, 128), 128)
            normed[:, cols] = down[part].T

    own_rows = pl.ds(pl.multiple_of(me.t * 16, 16), 16)
    for cols, total in reduce_rows(
        me, share, bufs_one, sems_one, share_one, lambda: turn_out(0, 32), lambda: None, pump
    ):
        middle[:, cols] = (h_v[own_rows, cols].astype(F32) + total).astype(BF16)
    field[me.x, me.zh, me.y] = norm_rows(middle[...].astype(F32), gain_two[...])

    spot = field.at[me.x, me.zh, me.y]
    swap = remote(spot, spot, x_s, x_r, me.across())
    gather_rows(me, field, swap, (a_s, a_r, b_s, b_r), pump)
    pump(20 - done[0])
    r_u.cores()
    r_u.complete()

    for part in range(8):
        rows = field[:, :, :, :, part * 512 : part * 512 + 512].reshape(512, 512)
        block = up[part * 4 : part * 4 + 4].reshape(512, 512)
        product = jnp.dot(rows, block, preferred_element_type=F32)
        if part == 0:
            acc[...] = product
        else:
            acc[...] += product

    @pl.loop(0, 8)
    def _(part):
        rows = pl.ds(pl.multiple_of(part * 64, 64), 64)
        values = acc[rows, :]
        act[rows, :] = (0.5 * values * (1.0 + lax.erf(values * math.sqrt(0.5)))).astype(BF16)

    r_d.cores()
    r_d.complete()

    for cols, total in reduce_rows(
        me, share, bufs_two, sems_two, share_two, lambda: turn_down(0, 16), lambda: turn_down(16, 32)
    ):
        result[:, cols] = (middle[:, cols].astype(F32) + total).astype(BF16)
    for batch in range(4):
        r_d.sent(batch)
    for relay in (r_q, r_u, r_d):
        relay.drain()


def layer(hidden, seg, gain_one, gain_two, qkv, out, up, down):
    any_spec = pl.BlockSpec(memory_space=pl.ANY)
    vmem = pl.BlockSpec(memory_space=pltpu.VMEM)
    dma = pltpu.SemaphoreType.DMA
    bufs_one, sems_one = reduce_scratch()
    bufs_two, sems_two = reduce_scratch()
    def relay_sems(parts):
        one, many = dma((8,)), dma((parts, 8))
        return [dma((4,)), dma(()), one, many, many, one, one, many, many]

    return pl.pallas_call(
        layer_kernel,
        out_shape=(
            pltpu.VMEM((16, D), BF16),
            pltpu.VMEM((512, HD), BF16),
            pltpu.VMEM((512, HD), BF16),
            pltpu.VMEM((4, 32, 128, HD), BF16),
            pltpu.VMEM((HD, D), BF16),
            pltpu.VMEM((32, 128, 512), BF16),
            pltpu.VMEM((512, D), BF16),
        ),
        in_specs=[any_spec, vmem, vmem, vmem] + [any_spec] * 4,
        out_specs=[vmem] * 7,
        scratch_shapes=[
            pltpu.VMEM((3, 32, 4096), F32),
            pltpu.VMEM((32, 4096), F32),
            pltpu.VMEM((32, 16384), F32),
            pltpu.VMEM((32, 16384), F32),
            pltpu.VMEM((512, D), BF16),
            pltpu.VMEM((32, 4, 32, 128), BF16),
            pltpu.VMEM((32, 32, 512), BF16),
            pltpu.VMEM((32, 32, 512), BF16),
            pltpu.VMEM((32, 128, 512), BF16),
            pltpu.VMEM((4, 2, 4, 16, D), BF16),
            pltpu.VMEM((4, 2, 4, 16, D), BF16),
            pltpu.VMEM((512, 512), F32),
            pltpu.VMEM((512, HD), BF16),
            pltpu.VMEM((512, HD), BF16),
            pltpu.VMEM((512, 512), BF16),
            pltpu.VMEM((16, D), BF16),
            dma((5,)),
        ]
        + relay_sems(2)
        + relay_sems(1)
        + relay_sems(1)
        + bufs_one
        + sems_one
        + bufs_two
        + sems_two
        + [dma((2, 2, 2, 2))] * 4
        + [dma(()), dma(())],
        compiler_params=pltpu.CompilerParams(
            collective_id=0, has_side_effects=True, vmem_limit_bytes=46 << 20
        ),
        name="layer",
    )(hidden, seg.reshape(1, 512), gain_one, gain_two, qkv, out, up, down)


def store_kernel(*refs):
    sem = refs[14]
    copies = [
        pltpu.make_async_copy(refs[k].at[pl.ds(0, refs[7 + k].shape[0])], refs[7 + k], sem.at[k])
        for k in range(7)
    ]
    for copy in copies:
        copy.start()
    for copy in copies:
        copy.wait()


def store(values):
    any_spec = pl.BlockSpec(memory_space=pl.ANY)
    vmem = pl.BlockSpec(memory_space=pltpu.VMEM)
    return pl.pallas_call(
        store_kernel,
        out_shape=[
            jax.ShapeDtypeStruct((3,) + value.shape[1:] if k == 3 else value.shape, value.dtype)
            for k, value in enumerate(values)
        ],
        in_specs=[any_spec] * 7,
        out_specs=[any_spec] * 7,
        scratch_shapes=[pltpu.SemaphoreType.DMA((7,))],
        compiler_params=pltpu.CompilerParams(vmem_limit_bytes=1 << 20),
        name="store",
    )(*values)


def shards(
    hidden, segment_ids, first_gain, second_gain, qkv_master, out_master, up_master, down_master
):
    made = layer(
        hidden,
        segment_ids,
        first_gain.reshape(1, D),
        second_gain.reshape(1, D),
        qkv_master.transpose(1, 0, 2),
        out_master.T,
        up_master,
        down_master.T,
    )
    new_hidden, keys, values, qkv, out_block, up, down_block = store(made)
    return (
        new_hidden,
        keys,
        values,
        qkv.reshape(3, D, HD).transpose(1, 0, 2),
        out_block,
        up.reshape(D, 512),
        down_block,
    )


def solution(mesh):
    in_specs = (
        P("dp", None),
        P("dp"),
        P(),
        P(),
        P(("dp", "tensor"), None, None),
        P(None, ("dp", "tensor")),
        P(("dp", "tensor"), None),
        P(None, ("dp", "tensor")),
    )
    out_specs = (
        P(("dp", "tensor"), None),
        P("dp", "tensor"),
        P("dp", "tensor"),
        P(None, None, "tensor"),
        P("tensor", None),
        P(None, "tensor"),
        P("tensor", None),
    )
    return jax.shard_map(shards, mesh=mesh, in_specs=in_specs, out_specs=out_specs, check_vma=False)
```

```python
import math

import jax
import jax.numpy as jnp
from jax import lax
from jax.experimental import pallas as pl
from jax.experimental.pallas import tpu as pltpu
from jax.sharding import PartitionSpec as P

D = 4096
HD = 128
EPSILON = 1e-05
MESH = pl.DeviceIdType.MESH
BF16 = jnp.bfloat16
F32 = jnp.float32


class Place:
    def __init__(self):
        self.dp = lax.axis_index("dp")
        self.t = lax.axis_index("tensor")
        self.zl = self.dp // 2
        self.core = self.dp % 2
        self.x = self.t // 8
        self.zh = (self.t // 4) % 2
        self.y = self.t % 4
        self.z_pair = (1 - self.zl) * 2 + self.core
        self.core_pair = self.zl * 2 + (1 - self.core)

    def near(self, axis, delta):
        if axis == "x":
            return (self.dp, ((self.x + delta) % 4) * 8 + self.zh * 4 + self.y)
        return (self.dp, self.x * 8 + self.zh * 4 + (self.y + delta) % 4)

    def across(self):
        return (self.dp, self.x * 8 + (1 - self.zh) * 4 + self.y)


def remote(src, dst, send_sem, recv_sem, device):
    return pltpu.make_async_remote_copy(
        src_ref=src,
        dst_ref=dst,
        send_sem=send_sem,
        recv_sem=recv_sem,
        device_id=device,
        device_id_type=MESH,
    )


def greet(barrier, device):
    pl.semaphore_signal(barrier, inc=1, device_id=device, device_id_type=MESH)


HALF = 2048
PART = 1024


def reduce_rows(me, share, bufs, sems, fill, while_first, while_second, pump=lambda count: None):
    ra, acc_a, rb, kept, last, last_half, rc = bufs
    sa, qa, sb, qb, sc, qc = sems
    axes = (("x", "y"), ("y", "x"))

    def chunk_a(f, s, q, h):
        cols = pl.ds(f * HALF + s * PART, PART)
        if f == 0:
            return share.at[q, h, :, :, cols]
        return share.at[:, h, q, :, cols]

    def position(f, level):
        return me.x if axes[f][level] == "x" else me.y

    class Direct:
        def __init__(self, s):
            self.s = s
            self.plan = [
                (
                    f,
                    [
                        remote(
                            kept.at[f, s, (position(f, 1) + delta) % 4],
                            rb.at[f, s, delta - 1],
                            sb.at[f, s, delta - 1],
                            qb.at[f, s, delta - 1],
                            me.near(axes[f][1], delta),
                        )
                        for delta in (1, 3, 2)
                    ],
                )
                for f in range(2)
            ]

        def start(self):
            for f, copies in self.plan:
                for copy in copies:
                    copy.start()

        def finalize(self):
            s = self.s
            for f, copies in self.plan:
                for copy in copies:
                    copy.wait_recv()
                total = kept[f, s, position(f, 1)].astype(F32)
                for k in range(3):
                    total = total + rb[f, s, k].astype(F32)
                last[f, s] = total
                last_half[f, s] = total.astype(BF16)

        def drain(self):
            for f, copies in self.plan:
                for copy in copies:
                    copy.wait_send()

    class Ring:
        def __init__(self, level, s, chunk, recv, acc, s_sem, r_sem):
            self.level, self.s, self.chunk, self.recv, self.acc = level, s, chunk, recv, acc
            self.plan = []
            for f in range(2):
                p = position(f, level)
                far = (p + 2) % 4
                for way in range(2):
                    delta = 1 - 2 * way
                    near = (p + delta) % 4
                    device = me.near(axes[f][level], delta)
                    copies = [
                        remote(src, recv.at[f, s, way, k], s_sem.at[f, s, way, k], r_sem.at[f, s, way, k], device)
                        for k, src in enumerate(
                            (chunk(f, s, far, way), chunk(f, s, near, 1 - way), acc.at[f, s, way])
                        )
                    ]
                    self.plan.append((f, way, near, copies))

        def start(self, k):
            for f, way, near, copies in self.plan:
                copies[k].start()

        def accumulate(self):
            s = self.s
            for f, way, near, copies in self.plan:
                copies[0].wait_recv()
                self.acc[f, s, way] = (
                    self.chunk(f, s, near, way)[...].astype(F32) + self.recv[f, s, way, 0].astype(F32)
                ).astype(BF16)
                copies[2].start()

        def finalize(self, store):
            s = self.s
            for f in range(2):
                p = position(f, self.level)
                both = [entry[3] for entry in self.plan if entry[0] == f]
                for h in range(2):
                    both[1 - h][1].wait_recv()
                    both[h][2].wait_recv()
                    total = (
                        self.chunk(f, s, p, h)[...].astype(F32)
                        + self.recv[f, s, h, 2].astype(F32)
                        + self.recv[f, s, 1 - h, 1].astype(F32)
                    )
                    store(f, s, h, total)

        def drain(self):
            for f, way, near, copies in self.plan:
                for copy in copies:
                    copy.wait_send()

    def store_a(f, s, h, total):
        kept[f, s, :, h] = total.astype(BF16)

    first = [Ring(0, s, chunk_a, ra, acc_a, sa, qa) for s in range(2)]
    second = [Direct(s) for s in range(2)]
    swaps = [
        [remote(last_half.at[f, s, 1 - me.zh], rc.at[f, s], sc.at[f, s], qc.at[f, s], me.across()) for f in range(2)]
        for s in range(2)
    ]
    fill(0)
    first[0].start(0)
    first[0].start(1)
    pump(1)
    fill(1)
    first[1].start(0)
    while_first()
    pump(1)
    first[0].accumulate()
    first[1].start(1)
    pump(1)
    first[1].accumulate()
    pump(1)
    first[0].finalize(store_a)
    second[0].start()
    pump(1)
    while_second()
    pump(1)
    first[1].finalize(store_a)
    second[1].start()
    second[0].finalize()
    for swap in swaps[0]:
        swap.start()
    second[1].finalize()
    for swap in swaps[1]:
        swap.start()
    sums = {}
    for s in range(2):
        for f in range(2):
            swaps[s][f].wait_recv()
            sums[f, s] = last[f, s, me.zh] + rc[f, s].astype(F32)
    for ring in first + second:
        ring.drain()
    for swap in swaps[0] + swaps[1]:
        swap.wait_send()
    return [(pl.ds(f * HALF + s * PART, PART), sums[f, s]) for f in range(2) for s in range(2)]


def reduce_scratch():
    dma = pltpu.SemaphoreType.DMA
    bufs = [
        pltpu.VMEM((2, 2, 2, 3, 4, 16, PART), BF16),
        pltpu.VMEM((2, 2, 2, 4, 16, PART), BF16),
        pltpu.VMEM((2, 2, 3, 2, 16, PART), BF16),
        pltpu.VMEM((2, 2, 4, 2, 16, PART), BF16),
        pltpu.VMEM((2, 2, 2, 16, PART), F32),
        pltpu.VMEM((2, 2, 2, 16, PART), BF16),
        pltpu.VMEM((2, 2, 16, PART), BF16),
    ]
    sems = [dma((2, 2, 2, 3))] * 2 + [dma((2, 2, 3))] * 2 + [dma((2, 2))] * 2
    return bufs, sems


class Relay:
    def __init__(self, me, source, stage, parts, sems):
        self.me, self.source, self.stage, self.parts = me, source, stage, parts
        self.s, self.own, self.r, self.zs, self.zr, self.cs, self.cr, self.ps, self.pr = sems

    def hop(self, turn):
        line = turn // 2
        return turn % 2, line + (line // 2) * (5 - 2 * line)

    def holder(self, step):
        me = self.me
        apart, dx = self.hop(step // 4)
        other = ((me.x + dx) % 4) * 8 + ((me.zh + apart) % 2) * 4 + (me.y + step) % 4
        return other, apart, ((me.zl + apart) % 2) * 2 + me.core

    def slot(self, turn):
        apart, dx = self.hop(turn)
        return apart * 4 + (self.me.x + 4 - dx) % 4

    def group(self, slot, flip_z, flip_c):
        me = self.me
        apart = slot // 4
        zl = (me.zl + apart + flip_z) % 2
        core = (me.core + flip_c) % 2
        return (zl * 2 + core) * 8 + (slot % 4) * 2 + (me.zh + apart) % 2

    def at(self, group, part=None, rows=None):
        ref = self.stage
        if len(ref.shape) == 4:
            span = slice(None) if part is None else self.parts[part]
            return ref.at[span, group] if rows is None else ref.at[span, group, rows]
        return ref.at[group] if rows is None else ref.at[group, rows]

    def own_piece(self):
        me = self.me
        mine = me.dp * 8 + me.x * 2 + me.zh
        return self.at(mine, rows=pl.ds(pl.multiple_of(me.y * 32, 32), 32))

    def send(self, batch):
        me = self.me

        def body(step, carry):
            other, apart, group = self.holder(step)
            remote(
                self.source.at[other],
                self.own_piece(),
                self.s.at[batch],
                self.r.at[apart * 4 + me.x],
                (group, other),
            ).start()
            return carry

        if batch == 0:
            pltpu.make_async_copy(self.source.at[me.t], self.own_piece(), self.own).start()
        lax.fori_loop(max(1, 8 * batch), 8 * batch + 8, body, 0)

    def sent(self, batch):
        pieces = self.source.at[pl.ds(0, 7 if batch == 0 else 8)]
        remote(pieces, pieces, self.s.at[batch], self.s.at[batch], (self.me.core_pair, self.me.t)).wait_send()

    def settle(self):
        pltpu.make_async_copy(self.source.at[self.me.t], self.own_piece(), self.own).wait()

    def wait_slot(self, slot):
        me = self.me
        group = self.group(slot, 0, 0)

        def got(count):
            ref = self.at(group, rows=pl.ds(0, count))
            remote(ref, ref, self.s.at[0], self.r.at[slot], (me.core_pair, me.t)).wait_recv()

        @pl.when(slot != me.x)
        def _():
            got(128)

        @pl.when(slot == me.x)
        def _():
            got(96)

    def to_z(self, slot, part=0):
        ref = self.at(self.group(slot, 0, 0), part)
        return remote(ref, ref, self.zs.at[part, slot], self.zr.at[part, slot], (self.me.z_pair, self.me.t))

    def to_core(self, slot):
        ref = self.at(self.group(slot, 0, 0))
        return remote(ref, ref, self.cs.at[slot], self.cr.at[slot], (self.me.core_pair, self.me.t))

    def pass_on(self, slot, part=0):
        ref = self.at(self.group(slot, 1, 0), part)
        return remote(ref, ref, self.ps.at[part, slot], self.pr.at[part, slot], (self.me.core_pair, self.me.t))

    def got(self, ref, sem):
        remote(ref, ref, self.s.at[0], sem, (self.me.core_pair, self.me.t)).wait_recv()

    def each(self, first, last, act):
        def body(turn, carry):
            act(self.slot(turn))
            return carry

        lax.fori_loop(first, last, body, 0)

    def forward(self, first, last):
        def act(slot):
            self.wait_slot(slot)
            self.to_z(slot).start()
            self.to_core(slot).start()

        self.each(first, last, act)

    def relay_on(self, first, last, part=0):
        def act(slot):
            self.got(self.at(self.group(slot, 1, 0), part), self.zr.at[part, slot])
            self.pass_on(slot, part).start()

        self.each(first, last, act)

    def cores(self):
        self.each(0, 8, lambda slot: self.got(self.at(self.group(slot, 0, 1)), self.cr.at[slot]))

    def complete(self, part=0):
        self.each(
            0, 8, lambda slot: self.got(self.at(self.group(slot, 1, 1), part), self.pr.at[part, slot])
        )

    def drain(self):
        def act(slot):
            self.to_core(slot).wait_send()
            for part in range(len(self.parts)):
                self.to_z(slot, part).wait_send()
                self.pass_on(slot, part).wait_send()

        self.each(0, 8, act)


def norm_rows(values, gain):
    center = values - jnp.mean(values, axis=-1, keepdims=True)
    spread = jnp.mean(center * center, axis=-1, keepdims=True)
    return (center * lax.rsqrt(spread + EPSILON) * gain).astype(BF16)


def gather_rows(me, field, swap, sems, pump):
    a_s, a_r, b_s, b_r = sems

    def direct(part):
        z = me.zh if part == 0 else 1 - me.zh
        plan = []
        for f, axis in ((0, "y"), (1, "x")):
            unit = field.at[me.x, z, me.y, :, pl.ds(f * HALF, HALF)]
            for delta in (1, 3, 2):
                at = (part, f, delta - 1)
                plan.append(remote(unit, unit, b_s.at[at], b_r.at[at], me.near(axis, delta)))
        return plan

    def view_a(f, part, q, half):
        z = me.zh if part == 0 else 1 - me.zh
        cols = pl.ds(f * HALF, HALF)
        some = slice(None) if half is None else pl.ds(2 * half, 2)
        if f == 0:
            return field.at[q, z, some, :, cols]
        return field.at[some, z, q, :, cols]

    def ring(part, view, axes, s_sem, r_sem):
        plan = []
        for f in range(2):
            axis = axes[f]
            p = me.x if axis == "x" else me.y
            for way in range(2):
                delta = 1 - 2 * way
                device = me.near(axis, delta)
                unit = view(f, part, p, None)
                came = view(f, part, (p + 4 - delta) % 4, way)
                at = (part, f, way)
                plan.append(
                    (
                        remote(unit, unit, s_sem.at[at + (0,)], r_sem.at[at + (0,)], device),
                        remote(came, came, s_sem.at[at + (1,)], r_sem.at[at + (1,)], device),
                    )
                )
        return plan

    def begin(plan):
        for whole, half in plan:
            whole.start()

    def turn(plan):
        for whole, half in plan:
            whole.wait_recv()
            half.start()

    def end(plan):
        for whole, half in plan:
            half.wait_recv()

    near = [direct(part) for part in range(2)]
    wide = [ring(part, view_a, ("x", "y"), a_s, a_r) for part in range(2)]
    swap.start()
    for copy in near[0]:
        copy.start()
    swap.wait_recv()
    for copy in near[1]:
        copy.start()
    pump(2)
    for part in range(2):
        for copy in near[part]:
            copy.wait_recv()
        begin(wide[part])
    pump(2)
    turn(wide[0])
    pump(1)
    turn(wide[1])
    pump(1)
    end(wide[0])
    end(wide[1])
    for copy in near[0] + near[1]:
        copy.wait_send()
    for plan in wide:
        for whole, half in plan:
            whole.wait_send()
            half.wait_send()
    swap.wait_send()


def attend(queries, keys, values, seg, slope, context):
    scale = 1.0 / math.sqrt(HD)
    for block in range(4):
        rows = pl.ds(block * 128, 128)
        reach = (block + 1) * 128
        cols = pl.ds(0, reach)
        scores = (
            lax.dot_general(
                queries[rows, :], keys[cols, :], (((1,), (1,)), ((), ())), preferred_element_type=F32
            )
            * scale
        )
        n = lax.broadcasted_iota(jnp.int32, (128, reach), 0) + block * 128
        p = lax.broadcasted_iota(jnp.int32, (128, reach), 1)
        scores = scores - slope * (n - p).astype(F32)
        own = jnp.broadcast_to(seg[:, rows], (128, 128)).T[:, 0:1]
        allowed = (own == seg[:, cols]) & (p <= n)
        scores = jnp.where(allowed, scores, -jnp.inf)
        highest = jnp.max(scores, axis=-1, keepdims=True)
        raised = jnp.exp(scores - highest)
        weights = (raised / jnp.sum(raised, axis=-1, keepdims=True)).astype(BF16)
        context[rows, :] = jnp.dot(weights, values[cols, :], preferred_element_type=F32).astype(BF16)


def layer_kernel(*refs):
    (hidden, seg, gain_one, gain_two, q_in, o_in, u_in, w_in) = refs[:8]
    (result, k_v, v_v, qo, turned, up, normed) = refs[8:15]
    rest = refs[15:]
    (q_f, o_f, u_f, w_f, h_v, sq, su, sw, down, field, share, acc, q_v, ctx, act, middle) = rest[:16]
    in_sem = rest[16]
    relay_sems = [rest[17 + 9 * k : 26 + 9 * k] for k in range(3)]
    rest = rest[44:]
    bufs_one, sems_one, bufs_two, sems_two = rest[:7], rest[7:13], rest[13:20], rest[20:26]
    a_s, a_r, b_s, b_r, x_s, x_r = rest[26:]
    me = Place()

    loads = [
        pltpu.make_async_copy(src, dst, in_sem.at[k])
        for k, (src, dst) in enumerate(
            ((q_in, q_f), (o_in, o_f), (u_in, u_f), (w_in, w_f), (hidden, h_v))
        )
    ]
    loads[0].start()
    loads[1].start()
    r_q = Relay(me, sq, qo, (pl.ds(0, 3), pl.ds(3, 1)), relay_sems[0])
    r_u = Relay(me, su, up, (None,), relay_sems[1])
    r_d = Relay(me, sw, down, (None,), relay_sems[2])

    barrier = pltpu.get_barrier_semaphore()

    def hello(step, carry):
        other, _, group = r_q.holder(step)
        greet(barrier, (group, other))
        return carry

    lax.fori_loop(1, 32, hello, 0)
    greet(barrier, (me.z_pair, me.t))
    greet(barrier, (me.core_pair, me.t))
    greet(barrier, me.across())
    loads[0].wait()
    loads[1].wait()
    for load in loads[2:]:
        load.start()

    @pl.loop(0, 32)
    def _(part):
        cols = pl.ds(pl.multiple_of(part * 128, 128), 128)
        sq[part, 0:3] = q_f[:, :, cols].astype(BF16)
        sq[part, 3] = o_f[:, cols].astype(BF16)

    pl.semaphore_wait(barrier, 34)
    r_q.send(0)

    def cast(source, target):
        @pl.loop(0, 32)
        def _(part):
            cols = pl.ds(pl.multiple_of(part * 512, 512), 512)
            target[part] = source[:, cols].astype(BF16)

    for batch in range(1, 4):
        r_q.send(batch)
    r_q.settle()
    r_q.forward(0, 2)
    loads[2].wait()
    cast(u_f, su)
    r_q.forward(2, 6)
    loads[3].wait()
    cast(w_f, sw)
    for batch in range(4):
        r_q.sent(batch)
    for batch in range(4):
        r_u.send(batch)
    r_q.forward(6, 8)
    r_q.each(0, 8, lambda slot: r_q.to_z(slot, 1).start())
    loads[4].wait()

    def passing(turn, carry):
        @pl.loop(0, 2)
        def _(part):
            rows = pl.ds(pl.multiple_of(turn * 64 + part * 32, 32), 32)
            normed[rows, :] = norm_rows(h_v[rows, :].astype(F32), gain_one[...])

        r_q.relay_on(turn, turn + 1)
        return carry

    lax.fori_loop(0, 4, passing, 0)
    for batch in range(4):
        passing(4 + batch, 0)
        r_u.sent(batch)
        r_d.send(batch)
    turns = [(relay, turn) for relay in (r_u, r_d) for turn in range(8)]
    done = [0]

    def pump(count):
        for _ in range(count):
            n = done[0]
            done[0] = n + 1
            if n < 16:
                relay, turn = turns[n]
                slot = relay.slot(turn)
                relay.wait_slot(slot)
                relay.to_z(slot).start()
                relay.to_core(slot).start()
            if n >= 4:
                relay, turn = turns[n - 4]
                relay.relay_on(turn, turn + 1)

    r_u.settle()
    pump(2)
    r_q.cores()
    r_q.complete()

    acc_q = acc.at[:, pl.ds(0, 384)]
    for part in range(4):
        cols = pl.ds(part * 1024, 1024)
        block = jnp.concatenate(
            [qo[k, part * 8 : part * 8 + 8].reshape(1024, 128) for k in range(3)], axis=1
        )
        product = jnp.dot(normed[:, cols], block, preferred_element_type=F32)
        if part == 0:
            acc_q[...] = product
        else:
            acc_q[...] += product
    pump(1)
    q_v[...] = acc[:, 0:128].astype(BF16)
    k_v[...] = acc[:, 128:256].astype(BF16)
    v_v[...] = acc[:, 256:384].astype(BF16)
    head = jnp.full((1, 128), me.t + 1, jnp.int32).astype(F32)
    attend(q_v, k_v, v_v, seg, jnp.exp2(-8.0 * head / (D // HD))[:, 0:1], ctx)
    pump(1)
    r_q.relay_on(0, 8, 1)
    r_q.complete(1)
    r_d.settle()

    def columns(i, part):
        return i % 2 + (i // 2) * 4 + 2 * part

    def share_one(part):
        @pl.loop(0, 4)
        def _(i):
            k = columns(i, part)
            block = qo[3, pl.ds(k * 4, 4)].reshape(512, 128)
            product = lax.dot_general(
                ctx[...], block, (((1,), (1,)), ((), ())), preferred_element_type=F32
            ).astype(BF16)
            cols = pl.ds(pl.multiple_of(k * 512, 512), 512)
            share[:, :, :, :, cols] = product.reshape(4, 2, 4, 16, 512)

    def share_two(part):
        @pl.loop(0, 4)
        def _(i):
            k = columns(i, part)
            block = down[pl.ds(k * 4, 4)].reshape(512, 512)
            product = lax.dot_general(
                act[...], block, (((1,), (1,)), ((), ())), preferred_element_type=F32
            ).astype(BF16)
            cols = pl.ds(pl.multiple_of(k * 512, 512), 512)
            share[:, :, :, :, cols] = product.reshape(4, 2, 4, 16, 512)

    pump(1)

    def turn_out(first, last):
        @pl.loop(first, last)
        def _(part):
            cols = pl.ds(pl.multiple_of(part * 128, 128), 128)
            turned[:, cols] = qo[3, part].T

    def turn_down(first, last):
        @pl.loop(first, last)
        def _(part):
            cols = pl.ds(pl.multiple_of(part * 128, 128), 128)
            normed[:, cols] = down[part].T

    own_rows = pl.ds(pl.multiple_of(me.t * 16, 16), 16)
    for cols, total in reduce_rows(
        me, share, bufs_one, sems_one, share_one, lambda: turn_out(0, 32), lambda: None, pump
    ):
        middle[:, cols] = (h_v[own_rows, cols].astype(F32) + total).astype(BF16)
    field[me.x, me.zh, me.y] = norm_rows(middle[...].astype(F32), gain_two[...])

    spot = field.at[me.x, me.zh, me.y]
    swap = remote(spot, spot, x_s, x_r, me.across())
    gather_rows(me, field, swap, (a_s, a_r, b_s, b_r), pump)
    pump(20 - done[0])
    r_u.cores()
    r_u.complete()

    for part in range(4):
        rows = field[:, :, :, :, part * 1024 : part * 1024 + 1024].reshape(512, 1024)
        block = up[part * 8 : part * 8 + 8].reshape(1024, 512)
        product = jnp.dot(rows, block, preferred_element_type=F32)
        if part == 0:
            acc[...] = product
        else:
            acc[...] += product

    @pl.loop(0, 8)
    def _(part):
        rows = pl.ds(pl.multiple_of(part * 64, 64), 64)
        values = acc[rows, :]
        act[rows, :] = (0.5 * values * (1.0 + lax.erf(values * math.sqrt(0.5)))).astype(BF16)

    r_d.cores()
    r_d.complete()

    for cols, total in reduce_rows(
        me, share, bufs_two, sems_two, share_two, lambda: turn_down(0, 16), lambda: turn_down(16, 32)
    ):
        result[:, cols] = (middle[:, cols].astype(F32) + total).astype(BF16)
    for batch in range(4):
        r_d.sent(batch)
    for relay in (r_q, r_u, r_d):
        relay.drain()


def layer(hidden, seg, gain_one, gain_two, qkv, out, up, down):
    any_spec = pl.BlockSpec(memory_space=pl.ANY)
    vmem = pl.BlockSpec(memory_space=pltpu.VMEM)
    dma = pltpu.SemaphoreType.DMA
    bufs_one, sems_one = reduce_scratch()
    bufs_two, sems_two = reduce_scratch()
    def relay_sems(parts):
        one, many = dma((8,)), dma((parts, 8))
        return [dma((4,)), dma(()), one, many, many, one, one, many, many]

    return pl.pallas_call(
        layer_kernel,
        out_shape=(
            pltpu.VMEM((16, D), BF16),
            pltpu.VMEM((512, HD), BF16),
            pltpu.VMEM((512, HD), BF16),
            pltpu.VMEM((4, 32, 128, HD), BF16),
            pltpu.VMEM((HD, D), BF16),
            pltpu.VMEM((32, 128, 512), BF16),
            pltpu.VMEM((512, D), BF16),
        ),
        in_specs=[any_spec, vmem, vmem, vmem] + [any_spec] * 4,
        out_specs=[vmem] * 7,
        scratch_shapes=[
            pltpu.VMEM((3, 32, 4096), F32),
            pltpu.VMEM((32, 4096), F32),
            pltpu.VMEM((32, 16384), F32),
            pltpu.VMEM((32, 16384), F32),
            pltpu.VMEM((512, D), BF16),
            pltpu.VMEM((32, 4, 32, 128), BF16),
            pltpu.VMEM((32, 32, 512), BF16),
            pltpu.VMEM((32, 32, 512), BF16),
            pltpu.VMEM((32, 128, 512), BF16),
            pltpu.VMEM((4, 2, 4, 16, D), BF16),
            pltpu.VMEM((4, 2, 4, 16, D), BF16),
            pltpu.VMEM((512, 512), F32),
            pltpu.VMEM((512, HD), BF16),
            pltpu.VMEM((512, HD), BF16),
            pltpu.VMEM((512, 512), BF16),
            pltpu.VMEM((16, D), BF16),
            dma((5,)),
        ]
        + relay_sems(2)
        + relay_sems(1)
        + relay_sems(1)
        + bufs_one
        + sems_one
        + bufs_two
        + sems_two
        + [dma((2, 2, 2, 2))] * 2
        + [dma((2, 2, 3))] * 2
        + [dma(()), dma(())],
        compiler_params=pltpu.CompilerParams(
            collective_id=0, has_side_effects=True, vmem_limit_bytes=46 << 20
        ),
        name="layer",
    )(hidden, seg.reshape(1, 512), gain_one, gain_two, qkv, out, up, down)


def store_kernel(*refs):
    sem = refs[14]
    copies = [
        pltpu.make_async_copy(refs[k].at[pl.ds(0, refs[7 + k].shape[0])], refs[7 + k], sem.at[k])
        for k in range(7)
    ]
    for copy in copies:
        copy.start()
    for copy in copies:
        copy.wait()


def store(values):
    any_spec = pl.BlockSpec(memory_space=pl.ANY)
    vmem = pl.BlockSpec(memory_space=pltpu.VMEM)
    return pl.pallas_call(
        store_kernel,
        out_shape=[
            jax.ShapeDtypeStruct((3,) + value.shape[1:] if k == 3 else value.shape, value.dtype)
            for k, value in enumerate(values)
        ],
        in_specs=[any_spec] * 7,
        out_specs=[any_spec] * 7,
        scratch_shapes=[pltpu.SemaphoreType.DMA((7,))],
        compiler_params=pltpu.CompilerParams(vmem_limit_bytes=1 << 20),
        name="store",
    )(*values)


def shards(
    hidden, segment_ids, first_gain, second_gain, qkv_master, out_master, up_master, down_master
):
    made = layer(
        hidden,
        segment_ids,
        first_gain.reshape(1, D),
        second_gain.reshape(1, D),
        qkv_master.transpose(1, 0, 2),
        out_master.T,
        up_master,
        down_master.T,
    )
    new_hidden, keys, values, qkv, out_block, up, down_block = store(made)
    return (
        new_hidden,
        keys,
        values,
        qkv.reshape(3, D, HD).transpose(1, 0, 2),
        out_block,
        up.reshape(D, 512),
        down_block,
    )


def solution(mesh):
    in_specs = (
        P("dp", None),
        P("dp"),
        P(),
        P(),
        P(("dp", "tensor"), None, None),
        P(None, ("dp", "tensor")),
        P(("dp", "tensor"), None),
        P(None, ("dp", "tensor")),
    )
    out_specs = (
        P(("dp", "tensor"), None),
        P("dp", "tensor"),
        P("dp", "tensor"),
        P(None, None, "tensor"),
        P("tensor", None),
        P(None, "tensor"),
        P("tensor", None),
    )
    return jax.shard_map(shards, mesh=mesh, in_specs=in_specs, out_specs=out_specs, check_vma=False)
```

```python
import math

import jax
import jax.numpy as jnp
from jax import lax
from jax.experimental import pallas as pl
from jax.experimental.pallas import tpu as pltpu
from jax.sharding import PartitionSpec as P

D = 4096
HD = 128
EPSILON = 1e-05
MESH = pl.DeviceIdType.MESH
BF16 = jnp.bfloat16
F32 = jnp.float32


class Place:
    def __init__(self):
        self.dp = lax.axis_index("dp")
        self.t = lax.axis_index("tensor")
        self.zl = self.dp // 2
        self.core = self.dp % 2
        self.x = self.t // 8
        self.zh = (self.t // 4) % 2
        self.y = self.t % 4
        self.z_pair = (1 - self.zl) * 2 + self.core
        self.core_pair = self.zl * 2 + (1 - self.core)

    def near(self, axis, delta):
        if axis == "x":
            return (self.dp, ((self.x + delta) % 4) * 8 + self.zh * 4 + self.y)
        return (self.dp, self.x * 8 + self.zh * 4 + (self.y + delta) % 4)

    def across(self):
        return (self.dp, self.x * 8 + (1 - self.zh) * 4 + self.y)


def remote(src, dst, send_sem, recv_sem, device):
    return pltpu.make_async_remote_copy(
        src_ref=src,
        dst_ref=dst,
        send_sem=send_sem,
        recv_sem=recv_sem,
        device_id=device,
        device_id_type=MESH,
    )


def greet(barrier, device):
    pl.semaphore_signal(barrier, inc=1, device_id=device, device_id_type=MESH)


HALF = 2048
PART = 1024


def reduce_rows(me, share, bufs, sems, fill, while_first, while_second, pump=lambda count: None):
    ra, acc_a, rb, kept, last, last_half, rc = bufs
    sa, qa, sb, qb, sc, qc = sems
    axes = (("x", "y"), ("y", "x"))

    def chunk_a(f, s, q, h):
        cols = pl.ds(f * HALF + s * PART, PART)
        if f == 0:
            return share.at[q, h, :, :, cols]
        return share.at[:, h, q, :, cols]

    def position(f, level):
        return me.x if axes[f][level] == "x" else me.y

    class Direct:
        def __init__(self, s):
            self.s = s
            self.plan = [
                (
                    f,
                    [
                        remote(
                            kept.at[f, s, (position(f, 1) + delta) % 4],
                            rb.at[f, s, delta - 1],
                            sb.at[f, s, delta - 1],
                            qb.at[f, s, delta - 1],
                            me.near(axes[f][1], delta),
                        )
                        for delta in (1, 3, 2)
                    ],
                )
                for f in range(2)
            ]

        def start(self):
            for f, copies in self.plan:
                for copy in copies:
                    copy.start()

        def finalize(self):
            s = self.s
            for f, copies in self.plan:
                for copy in copies:
                    copy.wait_recv()
                total = kept[f, s, position(f, 1)].astype(F32)
                for k in range(3):
                    total = total + rb[f, s, k].astype(F32)
                last[f, s] = total
                last_half[f, s] = total.astype(BF16)

        def drain(self):
            for f, copies in self.plan:
                for copy in copies:
                    copy.wait_send()

    class Ring:
        def __init__(self, level, s, chunk, recv, acc, s_sem, r_sem):
            self.level, self.s, self.chunk, self.recv, self.acc = level, s, chunk, recv, acc
            self.plan = []
            for f in range(2):
                p = position(f, level)
                far = (p + 2) % 4
                for way in range(2):
                    delta = 1 - 2 * way
                    near = (p + delta) % 4
                    device = me.near(axes[f][level], delta)
                    copies = [
                        remote(src, recv.at[f, s, way, k], s_sem.at[f, s, way, k], r_sem.at[f, s, way, k], device)
                        for k, src in enumerate(
                            (chunk(f, s, far, way), chunk(f, s, near, 1 - way), acc.at[f, s, way])
                        )
                    ]
                    self.plan.append((f, way, near, copies))

        def start(self, k):
            for f, way, near, copies in self.plan:
                copies[k].start()

        def accumulate(self):
            s = self.s
            for f, way, near, copies in self.plan:
                copies[0].wait_recv()
                self.acc[f, s, way] = (
                    self.chunk(f, s, near, way)[...].astype(F32) + self.recv[f, s, way, 0].astype(F32)
                ).astype(BF16)
                copies[2].start()

        def finalize(self, store):
            s = self.s
            for f in range(2):
                p = position(f, self.level)
                both = [entry[3] for entry in self.plan if entry[0] == f]
                for h in range(2):
                    both[1 - h][1].wait_recv()
                    both[h][2].wait_recv()
                    total = (
                        self.chunk(f, s, p, h)[...].astype(F32)
                        + self.recv[f, s, h, 2].astype(F32)
                        + self.recv[f, s, 1 - h, 1].astype(F32)
                    )
                    store(f, s, h, total)

        def drain(self):
            for f, way, near, copies in self.plan:
                for copy in copies:
                    copy.wait_send()

    def store_a(f, s, h, total):
        kept[f, s, :, h] = total.astype(BF16)

    first = [Ring(0, s, chunk_a, ra, acc_a, sa, qa) for s in range(2)]
    second = [Direct(s) for s in range(2)]
    swaps = [
        [remote(last_half.at[f, s, 1 - me.zh], rc.at[f, s], sc.at[f, s], qc.at[f, s], me.across()) for f in range(2)]
        for s in range(2)
    ]
    fill(0)
    first[0].start(0)
    first[0].start(1)
    pump(1)
    fill(1)
    first[1].start(0)
    while_first()
    pump(1)
    first[0].accumulate()
    first[1].start(1)
    pump(1)
    first[1].accumulate()
    pump(1)
    first[0].finalize(store_a)
    second[0].start()
    pump(1)
    while_second()
    first[1].finalize(store_a)
    second[1].start()
    second[0].finalize()
    for swap in swaps[0]:
        swap.start()
    second[1].finalize()
    for swap in swaps[1]:
        swap.start()
    sums = {}
    for s in range(2):
        for f in range(2):
            swaps[s][f].wait_recv()
            sums[f, s] = last[f, s, me.zh] + rc[f, s].astype(F32)
    for ring in first + second:
        ring.drain()
    for swap in swaps[0] + swaps[1]:
        swap.wait_send()
    return [(pl.ds(f * HALF + s * PART, PART), sums[f, s]) for f in range(2) for s in range(2)]


def reduce_scratch():
    dma = pltpu.SemaphoreType.DMA
    bufs = [
        pltpu.VMEM((2, 2, 2, 3, 4, 16, PART), BF16),
        pltpu.VMEM((2, 2, 2, 4, 16, PART), BF16),
        pltpu.VMEM((2, 2, 3, 2, 16, PART), BF16),
        pltpu.VMEM((2, 2, 4, 2, 16, PART), BF16),
        pltpu.VMEM((2, 2, 2, 16, PART), F32),
        pltpu.VMEM((2, 2, 2, 16, PART), BF16),
        pltpu.VMEM((2, 2, 16, PART), BF16),
    ]
    sems = [dma((2, 2, 2, 3))] * 2 + [dma((2, 2, 3))] * 2 + [dma((2, 2))] * 2
    return bufs, sems


class Relay:
    def __init__(self, me, source, stage, parts, sems):
        self.me, self.source, self.stage, self.parts = me, source, stage, parts
        self.s, self.own, self.r, self.zs, self.zr, self.cs, self.cr, self.ps, self.pr = sems

    def hop(self, turn):
        line = turn // 2
        return turn % 2, line + (line // 2) * (5 - 2 * line)

    def holder(self, step):
        me = self.me
        apart, dx = self.hop(step // 4)
        other = ((me.x + dx) % 4) * 8 + ((me.zh + apart) % 2) * 4 + (me.y + step) % 4
        return other, apart, ((me.zl + apart) % 2) * 2 + me.core

    def slot(self, turn):
        apart, dx = self.hop(turn)
        return apart * 4 + (self.me.x + 4 - dx) % 4

    def group(self, slot, flip_z, flip_c):
        me = self.me
        apart = slot // 4
        zl = (me.zl + apart + flip_z) % 2
        core = (me.core + flip_c) % 2
        return (zl * 2 + core) * 8 + (slot % 4) * 2 + (me.zh + apart) % 2

    def at(self, group, part=None, rows=None):
        ref = self.stage
        if len(ref.shape) == 4:
            span = slice(None) if part is None else self.parts[part]
            return ref.at[span, group] if rows is None else ref.at[span, group, rows]
        return ref.at[group] if rows is None else ref.at[group, rows]

    def own_piece(self):
        me = self.me
        mine = me.dp * 8 + me.x * 2 + me.zh
        return self.at(mine, rows=pl.ds(pl.multiple_of(me.y * 32, 32), 32))

    def send(self, batch):
        me = self.me

        def body(step, carry):
            other, apart, group = self.holder(step)
            remote(
                self.source.at[other],
                self.own_piece(),
                self.s.at[batch],
                self.r.at[apart * 4 + me.x],
                (group, other),
            ).start()
            return carry

        if batch == 0:
            pltpu.make_async_copy(self.source.at[me.t], self.own_piece(), self.own).start()
        lax.fori_loop(max(1, 8 * batch), 8 * batch + 8, body, 0)

    def sent(self, batch):
        pieces = self.source.at[pl.ds(0, 7 if batch == 0 else 8)]
        remote(pieces, pieces, self.s.at[batch], self.s.at[batch], (self.me.core_pair, self.me.t)).wait_send()

    def settle(self):
        pltpu.make_async_copy(self.source.at[self.me.t], self.own_piece(), self.own).wait()

    def wait_slot(self, slot):
        me = self.me
        group = self.group(slot, 0, 0)

        def got(count):
            ref = self.at(group, rows=pl.ds(0, count))
            remote(ref, ref, self.s.at[0], self.r.at[slot], (me.core_pair, me.t)).wait_recv()

        @pl.when(slot != me.x)
        def _():
            got(128)

        @pl.when(slot == me.x)
        def _():
            got(96)

    def to_z(self, slot, part=0):
        ref = self.at(self.group(slot, 0, 0), part)
        return remote(ref, ref, self.zs.at[part, slot], self.zr.at[part, slot], (self.me.z_pair, self.me.t))

    def to_core(self, slot):
        ref = self.at(self.group(slot, 0, 0))
        return remote(ref, ref, self.cs.at[slot], self.cr.at[slot], (self.me.core_pair, self.me.t))

    def pass_on(self, slot, part=0):
        ref = self.at(self.group(slot, 1, 0), part)
        return remote(ref, ref, self.ps.at[part, slot], self.pr.at[part, slot], (self.me.core_pair, self.me.t))

    def got(self, ref, sem):
        remote(ref, ref, self.s.at[0], sem, (self.me.core_pair, self.me.t)).wait_recv()

    def each(self, first, last, act):
        def body(turn, carry):
            act(self.slot(turn))
            return carry

        lax.fori_loop(first, last, body, 0)

    def forward(self, first, last):
        def act(slot):
            self.wait_slot(slot)
            self.to_z(slot).start()
            self.to_core(slot).start()

        self.each(first, last, act)

    def relay_on(self, first, last, part=0):
        def act(slot):
            self.got(self.at(self.group(slot, 1, 0), part), self.zr.at[part, slot])
            self.pass_on(slot, part).start()

        self.each(first, last, act)

    def cores(self):
        self.each(0, 8, lambda slot: self.got(self.at(self.group(slot, 0, 1)), self.cr.at[slot]))

    def complete(self, part=0):
        self.each(
            0, 8, lambda slot: self.got(self.at(self.group(slot, 1, 1), part), self.pr.at[part, slot])
        )

    def drain(self):
        def act(slot):
            self.to_core(slot).wait_send()
            for part in range(len(self.parts)):
                self.to_z(slot, part).wait_send()
                self.pass_on(slot, part).wait_send()

        self.each(0, 8, act)


def norm_rows(values, gain):
    center = values - jnp.mean(values, axis=-1, keepdims=True)
    spread = jnp.mean(center * center, axis=-1, keepdims=True)
    return (center * lax.rsqrt(spread + EPSILON) * gain).astype(BF16)


def gather_rows(me, field, swap, sems, pump, with_own):
    a_s, a_r, b_s, b_r = sems

    def direct(part):
        z = me.zh if part == 0 else 1 - me.zh
        plan = []
        for f, axis in ((0, "y"), (1, "x")):
            unit = field.at[me.x, z, me.y, :, pl.ds(f * HALF, HALF)]
            for delta in (1, 3, 2):
                at = (part, f, delta - 1)
                plan.append(remote(unit, unit, b_s.at[at], b_r.at[at], me.near(axis, delta)))
        return plan

    def view_a(f, part, q, half):
        z = me.zh if part == 0 else 1 - me.zh
        cols = pl.ds(f * HALF, HALF)
        some = slice(None) if half is None else pl.ds(2 * half, 2)
        if f == 0:
            return field.at[q, z, some, :, cols]
        return field.at[some, z, q, :, cols]

    def ring(part, view, axes, s_sem, r_sem):
        plan = []
        for f in range(2):
            axis = axes[f]
            p = me.x if axis == "x" else me.y
            for way in range(2):
                delta = 1 - 2 * way
                device = me.near(axis, delta)
                unit = view(f, part, p, None)
                came = view(f, part, (p + 4 - delta) % 4, way)
                at = (part, f, way)
                plan.append(
                    (
                        remote(unit, unit, s_sem.at[at + (0,)], r_sem.at[at + (0,)], device),
                        remote(came, came, s_sem.at[at + (1,)], r_sem.at[at + (1,)], device),
                    )
                )
        return plan

    def begin(plan):
        for whole, half in plan:
            whole.start()

    def turn(plan):
        for whole, half in plan:
            whole.wait_recv()
            half.start()

    def end(plan):
        for whole, half in plan:
            half.wait_recv()

    near = [direct(part) for part in range(2)]
    wide = [ring(part, view_a, ("x", "y"), a_s, a_r) for part in range(2)]
    swap.start()
    for copy in near[0]:
        copy.start()
    swap.wait_recv()
    for copy in near[1]:
        copy.start()
    pump(2)
    for part in range(2):
        for copy in near[part]:
            copy.wait_recv()
        begin(wide[part])
    pump(3)
    turn(wide[0])
    pump(1)
    turn(wide[1])
    pump(1)
    end(wide[0])
    with_own()
    end(wide[1])
    for copy in near[0] + near[1]:
        copy.wait_send()
    for plan in wide:
        for whole, half in plan:
            whole.wait_send()
            half.wait_send()
    swap.wait_send()


def attend(queries, keys, values, seg, slope, context):
    scale = 1.0 / math.sqrt(HD)
    for block in range(4):
        rows = pl.ds(block * 128, 128)
        reach = (block + 1) * 128
        cols = pl.ds(0, reach)
        scores = (
            lax.dot_general(
                queries[rows, :], keys[cols, :], (((1,), (1,)), ((), ())), preferred_element_type=F32
            )
            * scale
        )
        n = lax.broadcasted_iota(jnp.int32, (128, reach), 0) + block * 128
        p = lax.broadcasted_iota(jnp.int32, (128, reach), 1)
        scores = scores - slope * (n - p).astype(F32)
        own = jnp.broadcast_to(seg[:, rows], (128, 128)).T[:, 0:1]
        allowed = (own == seg[:, cols]) & (p <= n)
        scores = jnp.where(allowed, scores, -jnp.inf)
        highest = jnp.max(scores, axis=-1, keepdims=True)
        raised = jnp.exp(scores - highest)
        weights = (raised / jnp.sum(raised, axis=-1, keepdims=True)).astype(BF16)
        context[rows, :] = jnp.dot(weights, values[cols, :], preferred_element_type=F32).astype(BF16)


def layer_kernel(*refs):
    (hidden, seg, gain_one, gain_two, q_in, o_in, u_in, w_in) = refs[:8]
    (result, k_v, v_v, qo, turned, up, normed) = refs[8:15]
    rest = refs[15:]
    (q_f, o_f, u_f, w_f, h_v, sq, su, sw, down, field, share, acc, q_v, ctx, act, middle) = rest[:16]
    in_sem = rest[16]
    relay_sems = [rest[17 + 9 * k : 26 + 9 * k] for k in range(3)]
    rest = rest[44:]
    bufs_one, sems_one, bufs_two, sems_two = rest[:7], rest[7:13], rest[13:20], rest[20:26]
    a_s, a_r, b_s, b_r, x_s, x_r = rest[26:]
    me = Place()

    loads = [
        pltpu.make_async_copy(src, dst, in_sem.at[k])
        for k, (src, dst) in enumerate(
            ((q_in, q_f), (o_in, o_f), (u_in, u_f), (w_in, w_f), (hidden, h_v))
        )
    ]
    loads[0].start()
    loads[1].start()
    r_q = Relay(me, sq, qo, (pl.ds(0, 3), pl.ds(3, 1)), relay_sems[0])
    r_u = Relay(me, su, up, (None,), relay_sems[1])
    r_d = Relay(me, sw, down, (None,), relay_sems[2])

    barrier = pltpu.get_barrier_semaphore()

    def hello(step, carry):
        other, _, group = r_q.holder(step)
        greet(barrier, (group, other))
        return carry

    lax.fori_loop(1, 32, hello, 0)
    greet(barrier, (me.z_pair, me.t))
    greet(barrier, (me.core_pair, me.t))
    greet(barrier, me.across())
    loads[0].wait()
    loads[1].wait()
    for load in loads[2:]:
        load.start()

    @pl.loop(0, 32)
    def _(part):
        cols = pl.ds(pl.multiple_of(part * 128, 128), 128)
        sq[part, 0:3] = q_f[:, :, cols].astype(BF16)
        sq[part, 3] = o_f[:, cols].astype(BF16)

    pl.semaphore_wait(barrier, 34)
    r_q.send(0)

    def cast(source, target):
        @pl.loop(0, 32)
        def _(part):
            cols = pl.ds(pl.multiple_of(part * 512, 512), 512)
            target[part] = source[:, cols].astype(BF16)

    for batch in range(1, 4):
        r_q.send(batch)
    loads[2].wait()
    cast(u_f, su)
    loads[3].wait()
    cast(w_f, sw)
    r_q.settle()
    r_q.forward(0, 8)
    for batch in range(4):
        r_q.sent(batch)
    for batch in range(4):
        r_u.send(batch)
    r_q.each(0, 8, lambda slot: r_q.to_z(slot, 1).start())
    loads[4].wait()

    def passing(turn, carry):
        @pl.loop(0, 2)
        def _(part):
            rows = pl.ds(pl.multiple_of(turn * 64 + part * 32, 32), 32)
            normed[rows, :] = norm_rows(h_v[rows, :].astype(F32), gain_one[...])

        r_q.relay_on(turn, turn + 1)
        return carry

    lax.fori_loop(0, 4, passing, 0)
    for batch in range(4):
        passing(4 + batch, 0)
        r_u.sent(batch)
        r_d.send(batch)
    turns = [(relay, turn) for relay in (r_u, r_d) for turn in range(8)]
    done = [0]

    def pump(count):
        for _ in range(count):
            n = done[0]
            done[0] = n + 1
            if n < 16:
                relay, turn = turns[n]
                slot = relay.slot(turn)
                relay.wait_slot(slot)
                relay.to_z(slot).start()
                relay.to_core(slot).start()
            if n >= 4:
                relay, turn = turns[n - 4]
                relay.relay_on(turn, turn + 1)

    r_u.settle()
    pump(2)
    r_q.cores()
    r_q.complete()

    acc_q = acc.at[:, pl.ds(0, 384)]
    for part in range(4):
        cols = pl.ds(part * 1024, 1024)
        block = jnp.concatenate(
            [qo[k, part * 8 : part * 8 + 8].reshape(1024, 128) for k in range(3)], axis=1
        )
        product = jnp.dot(normed[:, cols], block, preferred_element_type=F32)
        if part == 0:
            acc_q[...] = product
        else:
            acc_q[...] += product
    pump(1)
    q_v[...] = acc[:, 0:128].astype(BF16)
    k_v[...] = acc[:, 128:256].astype(BF16)
    v_v[...] = acc[:, 256:384].astype(BF16)
    head = jnp.full((1, 128), me.t + 1, jnp.int32).astype(F32)
    attend(q_v, k_v, v_v, seg, jnp.exp2(-8.0 * head / (D // HD))[:, 0:1], ctx)
    pump(1)
    r_q.relay_on(0, 8, 1)
    r_q.complete(1)
    r_d.settle()

    def columns(i, part):
        return i % 2 + (i // 2) * 4 + 2 * part

    def share_one(part):
        @pl.loop(0, 4)
        def _(i):
            k = columns(i, part)
            block = qo[3, pl.ds(k * 4, 4)].reshape(512, 128)
            product = lax.dot_general(
                ctx[...], block, (((1,), (1,)), ((), ())), preferred_element_type=F32
            ).astype(BF16)
            cols = pl.ds(pl.multiple_of(k * 512, 512), 512)
            share[:, :, :, :, cols] = product.reshape(4, 2, 4, 16, 512)

    def share_two(part):
        @pl.loop(0, 4)
        def _(i):
            k = columns(i, part)
            block = down[pl.ds(k * 4, 4)].reshape(512, 512)
            product = lax.dot_general(
                act[...], block, (((1,), (1,)), ((), ())), preferred_element_type=F32
            ).astype(BF16)
            cols = pl.ds(pl.multiple_of(k * 512, 512), 512)
            share[:, me.zh, :, :, cols] = product[:256].reshape(4, 4, 16, 512)
            share[:, 1 - me.zh, :, :, cols] = product[256:].reshape(4, 4, 16, 512)

    pump(1)

    def turn_out(first, last):
        @pl.loop(first, last)
        def _(part):
            cols = pl.ds(pl.multiple_of(part * 128, 128), 128)
            turned[:, cols] = qo[3, part].T

    def turn_down(first, last):
        @pl.loop(first, last)
        def _(part):
            cols = pl.ds(pl.multiple_of(part * 128, 128), 128)
            normed[:, cols] = down[part].T

    own_rows = pl.ds(pl.multiple_of(me.t * 16, 16), 16)
    for cols, total in reduce_rows(
        me, share, bufs_one, sems_one, share_one, lambda: turn_out(0, 32), lambda: None, pump
    ):
        middle[:, cols] = (h_v[own_rows, cols].astype(F32) + total).astype(BF16)
    field[me.x, me.zh, me.y] = norm_rows(middle[...].astype(F32), gain_two[...])

    spot = field.at[me.x, me.zh, me.y]
    swap = remote(spot, spot, x_s, x_r, me.across())
    def hidden_units(part):
        z = me.zh if part == 0 else 1 - me.zh
        half = acc.at[pl.ds(part * 256, 256)]
        for k in range(4):
            rows = field[:, z, :, :, k * 1024 : k * 1024 + 1024].reshape(256, 1024)
            block = up[k * 8 : k * 8 + 8].reshape(1024, 512)
            product = jnp.dot(rows, block, preferred_element_type=F32)
            if k == 0:
                half[...] = product
            else:
                half[...] += product

        @pl.loop(0, 4)
        def _(step):
            rows = pl.ds(pl.multiple_of(part * 256 + step * 64, 64), 64)
            values = acc[rows, :]
            act[rows, :] = (0.5 * values * (1.0 + lax.erf(values * math.sqrt(0.5)))).astype(BF16)

    def with_own():
        r_u.cores()
        r_u.complete()
        hidden_units(0)

    gather_rows(me, field, swap, (a_s, a_r, b_s, b_r), pump, with_own)
    pump(20 - done[0])
    hidden_units(1)
    r_d.cores()
    r_d.complete()

    for cols, total in reduce_rows(
        me, share, bufs_two, sems_two, share_two, lambda: turn_down(0, 16), lambda: turn_down(16, 32)
    ):
        result[:, cols] = (middle[:, cols].astype(F32) + total).astype(BF16)
    for batch in range(4):
        r_d.sent(batch)
    for relay in (r_q, r_u, r_d):
        relay.drain()


def layer(hidden, seg, gain_one, gain_two, qkv, out, up, down):
    any_spec = pl.BlockSpec(memory_space=pl.ANY)
    vmem = pl.BlockSpec(memory_space=pltpu.VMEM)
    dma = pltpu.SemaphoreType.DMA
    bufs_one, sems_one = reduce_scratch()
    bufs_two, sems_two = reduce_scratch()
    def relay_sems(parts):
        one, many = dma((8,)), dma((parts, 8))
        return [dma((4,)), dma(()), one, many, many, one, one, many, many]

    return pl.pallas_call(
        layer_kernel,
        out_shape=(
            pltpu.VMEM((16, D), BF16),
            pltpu.VMEM((512, HD), BF16),
            pltpu.VMEM((512, HD), BF16),
            pltpu.VMEM((4, 32, 128, HD), BF16),
            pltpu.VMEM((HD, D), BF16),
            pltpu.VMEM((32, 128, 512), BF16),
            pltpu.VMEM((512, D), BF16),
        ),
        in_specs=[any_spec, vmem, vmem, vmem] + [any_spec] * 4,
        out_specs=[vmem] * 7,
        scratch_shapes=[
            pltpu.VMEM((3, 32, 4096), F32),
            pltpu.VMEM((32, 4096), F32),
            pltpu.VMEM((32, 16384), F32),
            pltpu.VMEM((32, 16384), F32),
            pltpu.VMEM((512, D), BF16),
            pltpu.VMEM((32, 4, 32, 128), BF16),
            pltpu.VMEM((32, 32, 512), BF16),
            pltpu.VMEM((32, 32, 512), BF16),
            pltpu.VMEM((32, 128, 512), BF16),
            pltpu.VMEM((4, 2, 4, 16, D), BF16),
            pltpu.VMEM((4, 2, 4, 16, D), BF16),
            pltpu.VMEM((512, 512), F32),
            pltpu.VMEM((512, HD), BF16),
            pltpu.VMEM((512, HD), BF16),
            pltpu.VMEM((512, 512), BF16),
            pltpu.VMEM((16, D), BF16),
            dma((5,)),
        ]
        + relay_sems(2)
        + relay_sems(1)
        + relay_sems(1)
        + bufs_one
        + sems_one
        + bufs_two
        + sems_two
        + [dma((2, 2, 2, 2))] * 2
        + [dma((2, 2, 3))] * 2
        + [dma(()), dma(())],
        compiler_params=pltpu.CompilerParams(
            collective_id=0, has_side_effects=True, vmem_limit_bytes=46 << 20
        ),
        name="layer",
    )(hidden, seg.reshape(1, 512), gain_one, gain_two, qkv, out, up, down)


def store_kernel(*refs):
    sem = refs[14]
    copies = [
        pltpu.make_async_copy(refs[k].at[pl.ds(0, refs[7 + k].shape[0])], refs[7 + k], sem.at[k])
        for k in range(7)
    ]
    for copy in copies:
        copy.start()
    for copy in copies:
        copy.wait()


def store(values):
    any_spec = pl.BlockSpec(memory_space=pl.ANY)
    vmem = pl.BlockSpec(memory_space=pltpu.VMEM)
    return pl.pallas_call(
        store_kernel,
        out_shape=[
            jax.ShapeDtypeStruct((3,) + value.shape[1:] if k == 3 else value.shape, value.dtype)
            for k, value in enumerate(values)
        ],
        in_specs=[any_spec] * 7,
        out_specs=[any_spec] * 7,
        scratch_shapes=[pltpu.SemaphoreType.DMA((7,))],
        compiler_params=pltpu.CompilerParams(vmem_limit_bytes=1 << 20),
        name="store",
    )(*values)


def shards(
    hidden, segment_ids, first_gain, second_gain, qkv_master, out_master, up_master, down_master
):
    made = layer(
        hidden,
        segment_ids,
        first_gain.reshape(1, D),
        second_gain.reshape(1, D),
        qkv_master.transpose(1, 0, 2),
        out_master.T,
        up_master,
        down_master.T,
    )
    new_hidden, keys, values, qkv, out_block, up, down_block = store(made)
    return (
        new_hidden,
        keys,
        values,
        qkv.reshape(3, D, HD).transpose(1, 0, 2),
        out_block,
        up.reshape(D, 512),
        down_block,
    )


def solution(mesh):
    in_specs = (
        P("dp", None),
        P("dp"),
        P(),
        P(),
        P(("dp", "tensor"), None, None),
        P(None, ("dp", "tensor")),
        P(("dp", "tensor"), None),
        P(None, ("dp", "tensor")),
    )
    out_specs = (
        P(("dp", "tensor"), None),
        P("dp", "tensor"),
        P("dp", "tensor"),
        P(None, None, "tensor"),
        P("tensor", None),
        P(None, "tensor"),
        P("tensor", None),
    )
    return jax.shard_map(shards, mesh=mesh, in_specs=in_specs, out_specs=out_specs, check_vma=False)
```
